32 devices in a mesh: dp: 2 (over core), expert: 4 (over y, x), tensor: 4 (over z).
Axes of the slice: x: 2, y: 2, z: 4, core: 2. Of those that a mesh axis runs over, the one named last changes fastest.
Arguments:
- grad_out: bfloat16 [1024, 3584], P(('dp', 'expert')), may hold values from -6 to 6
- layer_in: bfloat16 [1024, 3584], P(('dp', 'expert')), may hold values from -6 to 6
- routes: int32 [1024, 8], P(('dp', 'expert')), may hold values from 0 to 255, as said below
- combine: float32 [1024, 8], P(('dp', 'expert')), may hold values from 0.2 to 1
- gate_weight: bfloat16 [4, 3584, 1024], P('expert', 'dp', 'tensor'), may hold values from -0.09375 to 0.09375
- up_weight: bfloat16 [4, 3584, 1024], P('expert', 'dp', 'tensor'), may hold values from -0.09375 to 0.09375
- down_weight: bfloat16 [4, 1024, 3584], P('expert', 'tensor', 'dp'), may hold values from -0.1875 to 0.1875
Outputs:
- grad_in: bfloat16 [1024, 3584], P(('dp', 'expert'))
- grad_gate: bfloat16 [4, 3584, 1024], P('expert', 'dp', 'tensor')
- grad_up: bfloat16 [4, 3584, 1024], P('expert', 'dp', 'tensor')
- grad_down: bfloat16 [4, 1024, 3584], P('expert', 'tensor', 'dp')
The draws below stay inside these ranges and needn't reach their ends.
Inputs may be any that keep to these rules, and one draw needn't show every extreme that they name: `routes`: each row names 8 different experts. In every block of 128 tokens (the tokens of one device) each expert below 4 is named by 1 to 8 tokens, and one such expert, the same for all blocks of a draw, is named by exactly 8 tokens of every block.
All inputs are finite; a program needn't handle non-finite values.
Results may differ from the reference program's by a relative error of at most 0.011.
Values may be sent and summed in bfloat16 or wider, within the bound.
A program may use at most 128 MiB of HBM per device.

```python
import jax
import jax.numpy as jnp
from jax import lax

D = 3584
FF = 1024
ROUTED = 256
TOP = 8
TOK_DEV = 128
CAP = 8
EXPERTS = 4
TOKENS = 1024
N_DP = 2
N_EXPERT = 4
N_TENSOR = 4


def draw_routes(key, part):
    blocks = TOKENS // TOK_DEV
    subkeys = jax.random.split(jax.random.fold_in(key, 17), 5)
    labels = jnp.arange(EXPERTS, dtype=jnp.int32)
    lowest = max(CAP // 3, 1)
    counts = jax.random.randint(subkeys[0], (blocks, EXPERTS), lowest, CAP + 1).astype(jnp.int32)
    fullest = jax.random.randint(subkeys[1], (), 0, EXPERTS).astype(jnp.int32)
    counts = jnp.where(labels[None, :] == fullest, CAP, counts).astype(jnp.int32)
    residue = labels % TOP
    earlier = ((residue[:, None] == residue[None, :]) & (labels[:, None] < labels[None, :])).astype(jnp.int32)
    starts = jnp.sum(counts[:, :, None] * earlier[None, :, :], axis=1).astype(jnp.int32)
    scores = jax.random.randint(subkeys[2], (blocks, TOP, TOK_DEV), 0, 2 ** 20).astype(jnp.int32) * TOK_DEV + jnp.arange(TOK_DEV, dtype=jnp.int32)
    ranking = jnp.argsort(jnp.argsort(scores, axis=2), axis=2).astype(jnp.int32)
    rank_expert = jnp.take(ranking, residue, axis=1)
    inside = (rank_expert >= starts[:, :, None]) & (rank_expert < (starts + counts)[:, :, None])
    member = (residue[:, None] == jnp.arange(TOP, dtype=jnp.int32)[None, :]).astype(jnp.int32)
    inside_ints = jnp.transpose(inside.astype(jnp.int32), (0, 2, 1))
    found_one = jnp.sum(inside_ints[:, :, :, None] * member[None, None, :, :], axis=2)
    chosen_ids = jnp.sum((inside_ints * labels[None, None, :])[:, :, :, None] * member[None, None, :, :], axis=2)
    spare_ids = ROUTED - EXPERTS
    offset = jax.random.randint(subkeys[3], (blocks, TOK_DEV, 1), 0, spare_ids).astype(jnp.int32)
    others = EXPERTS + (offset + jnp.arange(TOP, dtype=jnp.int32)[None, None, :]) % spare_ids
    expert_ids = jnp.where(found_one > 0, chosen_ids, others).astype(jnp.int32)
    order_scores = jax.random.randint(subkeys[4], (blocks, TOK_DEV, TOP), 0, 2 ** 20).astype(jnp.int32) * TOP + jnp.arange(TOP, dtype=jnp.int32)
    shuffle = jnp.argsort(order_scores, axis=2)
    expert_ids = jnp.take_along_axis(expert_ids, shuffle, axis=2)
    return expert_ids.reshape(TOKENS, TOP).astype(jnp.int32)


def shard_levels(key, extent, shards, smallest, largest):
    level, own = 1.0, jax.random.fold_in(key, 6)
    for dim, parts in shards:
        heights = jnp.exp(jax.random.uniform(jax.random.fold_in(own, dim), (parts,), jnp.float32, smallest / len(shards), largest / len(shards)))
        level = level * jnp.repeat(heights, extent[dim] // parts).reshape([-1 if axis == dim else 1 for axis in range(len(extent))])
    return level


def centred(key, extent, spread, reach, cuts=(), kind=jnp.bfloat16):
    result = spread * jax.random.normal(key, extent, jnp.float32)
    if cuts:
        result = result * shard_levels(key, extent, cuts, -0.22, 0.18)
    return jnp.clip(result, -reach, reach).astype(kind)


def setup_inputs(seed: int = 0) -> dict:
    arg_keys = jax.random.split(jax.random.key(seed), 8)
    return {
        "grad_out": centred(arg_keys[0], (TOKENS, D), 1.0, 6.0, ((0, 8),)),
        "layer_in": centred(arg_keys[1], (TOKENS, D), 1.0, 6.0, ((0, 8),)),
        "routes": draw_routes(jax.random.fold_in(arg_keys[7], 71), 0),
        "combine": jnp.clip(0.2 + 0.8 * jax.random.uniform(arg_keys[3], (TOKENS, TOP), jnp.float32) ** shard_levels(arg_keys[3], (TOKENS, TOP), ((0, 8),), -0.2, 0.2), 0.2, 1.0),
        "gate_weight": centred(arg_keys[4], (EXPERTS, D, FF), D ** -0.5, 0.09375, ((0, 4), (1, 2), (2, 4))),
        "up_weight": centred(arg_keys[5], (EXPERTS, D, FF), D ** -0.5, 0.09375, ((0, 4), (1, 2), (2, 4))),
        "down_weight": centred(arg_keys[6], (EXPERTS, FF, D), FF ** -0.5, 0.1875, ((0, 4), (1, 4), (2, 2))),
    }


def expert_backward(in_rows, grad_rows, gate_w, up_w, down_w):
    gate = jnp.dot(in_rows, gate_w, preferred_element_type=jnp.float32)
    up = jnp.dot(in_rows, up_w, preferred_element_type=jnp.float32)
    sigma = jax.nn.sigmoid(gate)
    silu_gate = gate * sigma
    act = (silu_gate * up).astype(jnp.bfloat16)
    dhid = lax.dot_general(grad_rows, down_w, (((1,), (1,)), ((), ())), preferred_element_type=jnp.float32)
    d_up = (dhid * silu_gate).astype(jnp.bfloat16)
    d_gate = (dhid * up * sigma * (1.0 + gate * (1.0 - sigma))).astype(jnp.bfloat16)
    return act, d_gate, d_up


def reference(grad_out, layer_in, routes, combine, gate_weight, up_weight, down_weight):
    experts = gate_weight.shape[0]
    tokens, width = grad_out.shape
    blocks = tokens // TOK_DEV
    labels = jnp.arange(experts, dtype=jnp.int32)
    hits = routes[:, :, None] == labels[None, None, :]
    chosen = jnp.sum(hits, axis=1, dtype=jnp.int32)
    per_block = chosen.reshape(blocks, TOK_DEV, experts)
    before = (jnp.cumsum(per_block, axis=1) - per_block).reshape(tokens, experts).astype(jnp.int32)
    block_of = jnp.arange(tokens, dtype=jnp.int32) // TOK_DEV
    slot_of = (labels[None, :] * blocks + block_of[:, None]) * CAP + before
    dump_row = experts * blocks * CAP
    target = jnp.where(chosen > 0, slot_of, dump_row).astype(jnp.int32)
    token_ids = jnp.broadcast_to(jnp.arange(tokens, dtype=jnp.int32)[:, None] + 1, target.shape)
    owner = jnp.zeros((dump_row + 1,), jnp.int32).at[target.reshape(-1)].set(token_ids.reshape(-1))[:dump_row] - 1
    scale_of = jnp.sum(jnp.where(hits, combine[:, :, None], jnp.zeros((), jnp.float32)), axis=1)
    factor = jnp.zeros((dump_row + 1,), jnp.float32).at[target.reshape(-1)].set(scale_of.reshape(-1))[:dump_row]
    owner = owner.reshape(experts, blocks * CAP)
    factor = factor.reshape(experts, blocks * CAP)
    group_width = FF // N_TENSOR
    replica_rows = N_EXPERT * CAP

    def one_expert(items):
        owner_row, factor_row, gate_w, up_w, down_w = items
        valid = owner_row >= 0
        safe = jnp.maximum(owner_row, 0)
        in_rows = jnp.where(valid[:, None], layer_in[safe], jnp.zeros((), jnp.bfloat16))
        grad_rows = (grad_out[safe].astype(jnp.float32) * factor_row[:, None]).astype(jnp.bfloat16)
        act, d_gate, d_up = expert_backward(in_rows, grad_rows, gate_w, up_w, down_w)
        row_total = jnp.zeros(in_rows.shape, jnp.float32)
        for group in range(N_TENSOR):
            lo_col = group * group_width
            term = lax.dot_general(d_gate[:, lo_col:lo_col + group_width], gate_w[:, lo_col:lo_col + group_width], (((1,), (1,)), ((), ())), preferred_element_type=jnp.float32)
            term = term + lax.dot_general(d_up[:, lo_col:lo_col + group_width], up_w[:, lo_col:lo_col + group_width], (((1,), (1,)), ((), ())), preferred_element_type=jnp.float32)
            row_total = row_total + lax.optimization_barrier(term.astype(jnp.bfloat16)).astype(jnp.float32)
        gate_total = jnp.zeros(gate_w.shape, jnp.float32)
        up_total = jnp.zeros(up_w.shape, jnp.float32)
        down_total = jnp.zeros(down_w.shape, jnp.float32)
        for replica in range(N_DP):
            lo_row = replica * replica_rows
            rows_in = in_rows[lo_row:lo_row + replica_rows]
            part_gate = lax.dot_general(rows_in, d_gate[lo_row:lo_row + replica_rows], (((0,), (0,)), ((), ())), preferred_element_type=jnp.float32) * 0.25
            part_up = lax.dot_general(rows_in, d_up[lo_row:lo_row + replica_rows], (((0,), (0,)), ((), ())), preferred_element_type=jnp.float32) * 0.25
            part_down = lax.dot_general(act[lo_row:lo_row + replica_rows], grad_rows[lo_row:lo_row + replica_rows], (((0,), (0,)), ((), ())), preferred_element_type=jnp.float32) * 0.25
            gate_total = gate_total + lax.optimization_barrier(part_gate.astype(jnp.bfloat16)).astype(jnp.float32)
            up_total = up_total + lax.optimization_barrier(part_up.astype(jnp.bfloat16)).astype(jnp.float32)
            down_total = down_total + lax.optimization_barrier(part_down.astype(jnp.bfloat16)).astype(jnp.float32)
        return (row_total.astype(jnp.bfloat16), gate_total.astype(jnp.bfloat16), up_total.astype(jnp.bfloat16), down_total.astype(jnp.bfloat16))

    rows_all, grad_gate, grad_up, grad_down = lax.map(one_expert, (owner, factor, gate_weight, up_weight, down_weight))
    pair_pos = jnp.sum(jnp.where(hits, slot_of[:, None, :], 0), axis=2) + dump_row * (1 - jnp.sum(hits, axis=2, dtype=jnp.int32))
    pair_pos = pair_pos.astype(jnp.int32)
    row_table = jnp.concatenate([rows_all.reshape(dump_row, width), jnp.zeros((1, width), jnp.bfloat16)], axis=0)
    total = jnp.zeros((tokens, width), jnp.float32)
    for choice_index in range(TOP):
        total = total + row_table[pair_pos[:, choice_index]].astype(jnp.float32)
    return (total.astype(jnp.bfloat16), grad_gate, grad_up, grad_down)
```

```python
import jax
import jax.numpy as jnp
from jax import lax
from jax.experimental import pallas as pl
from jax.experimental.pallas import tpu as pltpu
from jax.sharding import PartitionSpec as P

CAP = 8
PICK_PARTS = 1
STORE_PARTS = 4
VMEM = 67043328
MESH = pl.DeviceIdType.MESH
F32 = jnp.float32
BF16 = jnp.bfloat16


def dot(a, b, ca, cb):
    return lax.dot_general(a, b, (((ca,), (cb,)), ((), ())), preferred_element_type=F32)


def cuts(extent, parts):
    tiles = extent // 128
    edges = [128 * ((tiles * c + parts - 1) // parts) for c in range(parts + 1)]
    return list(zip(edges[:-1], edges[1:]))


def partner(e, k, ne):
    out, bit = 0, 1
    while bit < ne:
        own = lax.rem(lax.div(e, bit), 2)
        out = out + bit * ((1 - own) if k & bit else own)
        bit *= 2
    return out


def group_ranges(ne):
    edges = sorted({0, 1, 3 * ne // 4, ne})
    return list(zip(edges[:-1], edges[1:]))


def make_kernel(nd, ne, nz, tokens, width, half, hidden, top):
    lanes = ne * CAP
    pick_cuts = cuts(half, PICK_PARTS)
    groups = group_ranges(ne)
    last = len(groups) - 1

    def kernel(
        go_hbm, li_hbm, routes_hbm, combine_hbm, gw_hbm, uw_hbm, dw_hbm,
        agbuf, pick_ref, gg_ref, gu_ref, gd_ref,
        go, li, routes, combine, gw, uw, dw, send, recv, psend, precv, rowg, terms, pads,
        ld_sem, d_send, d_recv, p_send, p_recv, r_send, r_recv, a_send, a_recv,
    ):
        d = lax.axis_index("dp")
        e = lax.axis_index("expert")
        z = lax.axis_index("tensor")
        peer = [partner(e, k, ne) for k in range(ne)]
        reducer = lax.div(z, nd) == d
        part = lax.rem(z, nd)

        loads = [
            pltpu.make_async_copy(li_hbm, li, ld_sem.at[0]),
            pltpu.make_async_copy(go_hbm, go, ld_sem.at[1]),
            pltpu.make_async_copy(gw_hbm.at[0], gw, ld_sem.at[2]),
            pltpu.make_async_copy(uw_hbm.at[0], uw, ld_sem.at[3]),
            pltpu.make_async_copy(dw_hbm.at[0], dw, ld_sem.at[4]),
            pltpu.make_async_copy(routes_hbm, routes, ld_sem.at[5]),
            pltpu.make_async_copy(combine_hbm, combine, ld_sem.at[6]),
        ]
        for i in (5, 6, 0, 1):
            loads[i].start()

        barrier = pltpu.get_barrier_semaphore()
        peers = 0
        for k in range(ne - 1, -1, -1):
            for j in range(nd):
                if j == 0 and k == 0:
                    continue
                pl.semaphore_signal(
                    barrier, inc=1, device_id=(lax.rem(d + j, nd), peer[k], z),
                    device_id_type=MESH,
                )
                peers += 1
        for r in range(1, nz):
            pl.semaphore_signal(
                barrier, inc=1, device_id=(d, e, lax.rem(z + r, nz)), device_id_type=MESH
            )
            peers += 1
        for i in (2, 3, 4):
            loads[i].start()

        row = lax.broadcasted_iota(jnp.int32, (lanes, tokens), 0)
        group = row // CAP
        slot = row - group * CAP
        label = jnp.zeros((lanes, tokens), jnp.int32)
        for k in range(ne):
            label = jnp.where(group == k, peer[k], label)
        chosen = jnp.zeros((lanes, tokens), F32)
        scale = jnp.zeros((lanes, tokens), F32)
        loads[5].wait()
        loads[6].wait()
        for c in range(top):
            hit = routes[c : c + 1, :] == label
            chosen = chosen + jnp.where(hit, 1.0, 0.0)
            scale = scale + jnp.where(hit, combine[c : c + 1, :], 0.0)
        row_id = lax.broadcasted_iota(jnp.int32, (tokens, tokens), 0)
        col_id = lax.broadcasted_iota(jnp.int32, (tokens, tokens), 1)
        upper = jnp.where(row_id < col_id, 1.0, 0.0).astype(BF16)
        before = dot(chosen.astype(BF16), upper, 1, 0)
        keep = jnp.logical_and(chosen > 0.0, before == slot.astype(F32))
        pick_f = jnp.where(keep, 1.0, 0.0)
        pick = pick_f.astype(BF16)
        factor = jnp.sum(pick_f * scale, axis=1, keepdims=True)
        pick_ref[...] = pick

        loads[0].wait()
        loads[1].wait()

        def dispatch(k, j, c):
            lo, hi = pick_cuts[c]
            span = pl.ds(lo, hi - lo)
            return pltpu.make_async_remote_copy(
                src_ref=send.at[k, j, :, span], dst_ref=recv.at[k, d, :, span],
                send_sem=d_send.at[k, j, c], recv_sem=d_recv.at[k, d, c],
                device_id=(lax.rem(d + j, nd), peer[k], z), device_id_type=MESH,
            )

        late = []
        entered = False
        for j in range(nd - 1, -1, -1):
            for c, (lo, hi) in enumerate(pick_cuts):
                dj = lax.rem(d + j, nd)
                span = pl.ds(pl.multiple_of(dj * half + lo, 128), hi - lo)
                in_pick = dot(pick, li[:, span], 1, 0)
                gr_pick = dot(pick, go[:, span], 1, 0) * factor
                if not entered:
                    pl.semaphore_wait(barrier, peers)
                    entered = True
                for k in [*range(1, ne), 0]:
                    at = k * CAP
                    tile = jnp.concatenate(
                        [in_pick[at : at + CAP], gr_pick[at : at + CAP]], axis=0
                    ).astype(BF16)
                    if j == 0 and k == 0:
                        recv[0, d, :, lo:hi] = tile
                        continue
                    send[k, j, :, lo:hi] = tile
                    if k >= groups[-1][0]:
                        late.append((k, j, c))
                    else:
                        dispatch(k, j, c).start()
        for k, j, c in late:
            dispatch(k, j, c).start()
        for c in loads[2:5]:
            c.wait()

        def arrived(k, s):
            for c, (lo, hi) in enumerate(pick_cuts):
                ref = recv.at[k, s, :, pl.ds(lo, hi - lo)]
                pltpu.make_async_copy(ref, ref, d_recv.at[k, s, c]).wait()

        def take(v, which):
            n = v.shape[0] // (2 * CAP)
            return v.reshape(n, 2, CAP, hidden)[:, which].reshape(n * CAP, hidden)

        def exchange(g, j):
            lo, hi = (k * nd * CAP for k in groups[g])
            span = pl.ds(lo, hi - lo)
            return pltpu.make_async_remote_copy(
                src_ref=psend.at[:, span], dst_ref=precv.at[j - 1, :, span],
                send_sem=p_send.at[g, j - 1], recv_sem=p_recv.at[g, j - 1],
                device_id=(lax.rem(d + j, nd), e, z), device_id_type=MESH,
            )

        def project(g):
            k0, k1 = groups[g]
            for k in range(k0, k1):
                if k == 0:
                    for j in range(1, nd):
                        arrived(0, lax.rem(d + j, nd))
                else:
                    for s in range(nd):
                        arrived(k, s)
            x = recv[k0:k1].reshape((k1 - k0) * nd * 2 * CAP, half)
            sums = [
                take(dot(x, gw[...], 1, 0), 0),
                take(dot(x, uw[...], 1, 0), 0),
                take(dot(x, dw[...], 1, 1), 1),
            ]
            lo, hi = k0 * nd * CAP, k1 * nd * CAP
            for i, v in enumerate(sums):
                psend[i, lo:hi] = v.astype(BF16)
            for j in range(1, nd):
                exchange(g, j).start()
            return sums

        def term_copy(k, s):
            return pltpu.make_async_remote_copy(
                src_ref=rowg.at[k, s], dst_ref=terms.at[z, k],
                send_sem=r_send.at[k, s], recv_sem=r_recv.at[z, k],
                device_id=(s, peer[k], s * nd + d), device_id_type=MESH,
            )

        def is_own(s):
            return jnp.logical_and(d == s, z == s * nd + d)

        def finish(g, sums):
            k0, k1 = groups[g]
            lo, hi = k0 * nd * CAP, k1 * nd * CAP
            gate, up, dhid = sums
            for j in range(1, nd):
                exchange(g, j).wait_recv()
                gate = gate + precv[j - 1, 0, lo:hi].astype(F32)
                up = up + precv[j - 1, 1, lo:hi].astype(F32)
                dhid = dhid + precv[j - 1, 2, lo:hi].astype(F32)
            sigma = jax.nn.sigmoid(gate)
            silu = gate * sigma
            act = silu * up
            d_up = dhid * silu
            d_gate = dhid * up * sigma * (1.0 + gate * (1.0 - sigma))
            grad = dot(d_gate.astype(BF16), gw[...], 1, 1) + dot(d_up.astype(BF16), uw[...], 1, 1)
            grad = grad.reshape(k1 - k0, nd, CAP, half).astype(BF16)
            for k in range(k0, k1):
                for s in range(nd):
                    rowg[k, s] = grad[k - k0, s]
                    if k:
                        term_copy(k, s).start()
                        continue

                    @pl.when(is_own(s))
                    def _():
                        pltpu.make_async_copy(rowg.at[0, s], terms.at[z, 0], r_recv.at[z, 0]).start()

                    @pl.when(jnp.logical_not(is_own(s)))
                    def _():
                        term_copy(0, s).start()
            for i, v in enumerate((d_gate, d_up, act)):
                v = v.reshape((k1 - k0) * nd, CAP, hidden)
                zero = jnp.zeros_like(v)
                pair = [zero, v] if i == 2 else [v, zero]
                pads[i, k0 * nd : k1 * nd] = jnp.concatenate(pair, axis=1).astype(BF16)

        def gather(g, r):
            k0, k1 = groups[g]
            ref = agbuf.at[part, pl.ds(k0, k1 - k0)]
            return pltpu.make_async_remote_copy(
                src_ref=ref, dst_ref=ref,
                send_sem=a_send.at[g, r - 1], recv_sem=a_recv.at[g, part],
                device_id=(d, e, lax.rem(z + r, nz)), device_id_type=MESH,
            )

        def reduce(g):
            k0, k1 = groups[g]

            @pl.when(reducer)
            def _():
                for k in range(k0, k1):
                    for q in range(nz):
                        ref = terms.at[q, k]
                        pltpu.make_async_copy(ref, ref, r_recv.at[q, k]).wait()
                total = terms[0, k0:k1].astype(F32)
                for q in range(1, nz):
                    total = total + terms[q, k0:k1].astype(F32)
                agbuf[part, k0:k1] = total.astype(BF16)
                for r in range(1, nz):
                    gather(g, r).start()

        every = ne * nd * 2 * CAP

        def weight_grad(i):
            x = recv[...].reshape(every, half)
            v = pads[i].reshape(every, hidden)
            if i == 2:
                gd_ref[0] = (dot(v, x, 0, 0) * 0.25).astype(BF16)
            else:
                (gg_ref, gu_ref)[i][0] = (dot(x, v, 0, 0) * 0.25).astype(BF16)

        for g in range(len(groups)):
            sums = project(g)
            if g == last:
                for h in range(last - 1):
                    reduce(h)
            finish(g, sums)
        weight_grad(0)
        for h in range(max(last - 1, 0), last):
            reduce(h)
        weight_grad(1)
        weight_grad(2)
        reduce(last)

        for g, (k0, k1) in enumerate(groups):
            for h in range(nd):
                @pl.when(z != d * nd + h)
                def _():
                    ref = agbuf.at[h, pl.ds(k0, k1 - k0)]
                    pltpu.make_async_copy(ref, ref, a_recv.at[g, h]).wait()

        for k in range(ne):
            for j in range(nd):
                if j == 0 and k == 0:
                    continue
                for c in range(len(pick_cuts)):
                    dispatch(k, j, c).wait_send()
        for g in range(len(groups)):
            for j in range(1, nd):
                exchange(g, j).wait_send()
        for k in range(ne):
            for s in range(nd):
                if k:
                    term_copy(k, s).wait_send()
                else:
                    @pl.when(jnp.logical_not(is_own(s)))
                    def _():
                        term_copy(0, s).wait_send()

        @pl.when(reducer)
        def _():
            for g in range(len(groups)):
                for r in range(1, nz):
                    gather(g, r).wait_send()

    return kernel


def make_store(nd, lanes, half):
    parts = [(h, lo, hi) for h in range(nd) for lo, hi in cuts(half, STORE_PARTS // nd)]

    def kernel(agbuf, pick_ref, gg, gu, gd, out, gg_out, gu_out, gd_out, out_v, sem, out_sem):
        copies = [
            pltpu.make_async_copy(src, dst, sem.at[i])
            for i, (src, dst) in enumerate(((gg, gg_out), (gu, gu_out), (gd, gd_out)))
        ]
        for c in copies:
            c.start()
        pick = pick_ref[...]
        for i, (h, lo, hi) in enumerate(parts):
            got = agbuf[h, :, :, lo:hi].astype(F32).reshape(lanes, hi - lo).astype(BF16)
            span = pl.ds(h * half + lo, hi - lo)
            out_v[:, span] = dot(pick, got, 0, 0).astype(BF16)
            c = pltpu.make_async_copy(out_v.at[:, span], out.at[:, span], out_sem.at[i])
            c.start()
            copies.append(c)
        for c in copies:
            c.wait()

    return kernel, len(parts)


def body(grad_out, layer_in, routes, combine, gate_weight, up_weight, down_weight):
    nd = lax.axis_size("dp")
    ne = lax.axis_size("expert")
    nz = lax.axis_size("tensor")
    tokens, width = grad_out.shape
    top = routes.shape[1]
    half, hidden = gate_weight.shape[1:]
    lanes = ne * CAP
    groups = len(group_ranges(ne))
    kernel = make_kernel(nd, ne, nz, tokens, width, half, hidden, top)
    hbm = pl.BlockSpec(memory_space=pltpu.HBM)
    vmem = pl.BlockSpec(memory_space=pltpu.VMEM)
    dma = pltpu.SemaphoreType.DMA
    held = 2 * (nd * lanes * half + lanes * tokens + 3 * half * hidden)
    room = VMEM - held
    arrays = pl.pallas_call(
        kernel,
        out_shape=(
            pltpu.VMEM((nd, ne, CAP, half), BF16),
            pltpu.VMEM((lanes, tokens), BF16),
            pltpu.VMEM(gate_weight.shape, BF16),
            pltpu.VMEM(up_weight.shape, BF16),
            pltpu.VMEM(down_weight.shape, BF16),
        ),
        in_specs=[hbm] * 7,
        out_specs=(vmem,) * 5,
        scratch_shapes=[
            pltpu.VMEM((tokens, width), BF16),
            pltpu.VMEM((tokens, width), BF16),
            pltpu.VMEM((top, tokens), jnp.int32),
            pltpu.VMEM((top, tokens), F32),
            pltpu.VMEM((half, hidden), BF16),
            pltpu.VMEM((half, hidden), BF16),
            pltpu.VMEM((hidden, half), BF16),
            pltpu.VMEM((ne, nd, 2 * CAP, half), BF16),
            pltpu.VMEM((ne, nd, 2 * CAP, half), BF16),
            pltpu.VMEM((3, ne * nd * CAP, hidden), BF16),
            pltpu.VMEM((nd - 1, 3, ne * nd * CAP, hidden), BF16),
            pltpu.VMEM((ne, nd, CAP, half), BF16),
            pltpu.VMEM((nz, ne, CAP, half), BF16),
            pltpu.VMEM((3, ne * nd, 2 * CAP, hidden), BF16),
            dma((7,)),
            dma((ne, nd, PICK_PARTS)),
            dma((ne, nd, PICK_PARTS)),
            dma((groups, nd - 1)),
            dma((groups, nd - 1)),
            dma((ne, nd)),
            dma((nz, ne)),
            dma((groups, nz - 1)),
            dma((groups, nd)),
        ],
        compiler_params=pltpu.CompilerParams(
            collective_id=0, has_side_effects=True, vmem_limit_bytes=room
        ),
    )(grad_out, layer_in, routes.T, combine.T, gate_weight, up_weight, down_weight)
    store, parts = make_store(nd, lanes, half)
    return tuple(pl.pallas_call(
        store,
        out_shape=tuple(
            jax.ShapeDtypeStruct(v.shape, BF16)
            for v in (grad_out, gate_weight, up_weight, down_weight)
        ),
        in_specs=[vmem] * 5,
        out_specs=(hbm,) * 4,
        scratch_shapes=[pltpu.VMEM((tokens, width), BF16), dma((3,)), dma((parts,))],
        compiler_params=pltpu.CompilerParams(vmem_limit_bytes=16 * 2**20),
    )(*[pltpu.with_memory_space_constraint(a, pltpu.VMEM) for a in arrays]))


def solution(mesh):
    return jax.shard_map(
        body,
        mesh=mesh,
        in_specs=(
            P(("dp", "expert"), None),
            P(("dp", "expert"), None),
            P(("dp", "expert"), None),
            P(("dp", "expert"), None),
            P("expert", "dp", "tensor"),
            P("expert", "dp", "tensor"),
            P("expert", "tensor", "dp"),
        ),
        out_specs=(
            P(("dp", "expert"), None),
            P("expert", "dp", "tensor"),
            P("expert", "dp", "tensor"),
            P("expert", "tensor", "dp"),
        ),
        check_vma=False,
    )
```

```python
import jax
import jax.numpy as jnp
from jax import lax
from jax.experimental import pallas as pl
from jax.experimental.pallas import tpu as pltpu
from jax.sharding import PartitionSpec as P

CAP = 8
PICK_PARTS = 1
BACK_PARTS = 2
STORE_PARTS = 4
VMEM = 67043328
MESH = pl.DeviceIdType.MESH
F32 = jnp.float32
BF16 = jnp.bfloat16


def dot(a, b, ca, cb):
    return lax.dot_general(a, b, (((ca,), (cb,)), ((), ())), preferred_element_type=F32)


def cuts(extent, parts):
    tiles = extent // 128
    edges = [128 * ((tiles * c + parts - 1) // parts) for c in range(parts + 1)]
    return list(zip(edges[:-1], edges[1:]))


def partner(e, k, ne):
    out, bit = 0, 1
    while bit < ne:
        own = lax.rem(lax.div(e, bit), 2)
        out = out + bit * ((1 - own) if k & bit else own)
        bit *= 2
    return out


def group_ranges(ne):
    edges = sorted({0, 1, 3 * ne // 4, ne})
    return list(zip(edges[:-1], edges[1:]))


def make_kernel(nd, ne, nz, tokens, width, half, hidden, top):
    lanes = ne * CAP
    pick_cuts = cuts(half, PICK_PARTS)
    groups = group_ranges(ne)
    last = len(groups) - 1
    back_cuts = cuts(half, BACK_PARTS)

    def kernel(
        go_hbm, li_hbm, routes_hbm, combine_hbm, gw_hbm, uw_hbm, dw_hbm,
        agbuf, pick_ref, gg_ref, gu_ref, gd_ref,
        go, li, routes, combine, gw, uw, dw, dw_t, back_t, send, recv, psend, precv, rowg, terms, pads,
        ld_sem, d_send, d_recv, p_send, p_recv, r_send, r_recv, a_send, a_recv,
    ):
        d = lax.axis_index("dp")
        e = lax.axis_index("expert")
        z = lax.axis_index("tensor")
        peer = [partner(e, k, ne) for k in range(ne)]
        part = z - (nd * d)
        reducer = jnp.logical_and(part >= 0, part < nd)

        loads = [
            pltpu.make_async_copy(li_hbm, li, ld_sem.at[0]),
            pltpu.make_async_copy(go_hbm, go, ld_sem.at[1]),
            pltpu.make_async_copy(gw_hbm.at[0], gw, ld_sem.at[2]),
            pltpu.make_async_copy(uw_hbm.at[0], uw, ld_sem.at[3]),
            pltpu.make_async_copy(dw_hbm.at[0], dw, ld_sem.at[4]),
            pltpu.make_async_copy(routes_hbm, routes, ld_sem.at[5]),
            pltpu.make_async_copy(combine_hbm, combine, ld_sem.at[6]),
        ]
        barrier = pltpu.get_barrier_semaphore()
        peers = 0
        for k in range(ne - 1, -1, -1):
            for j in range(nd):
                if j == 0 and k == 0:
                    continue
                pl.semaphore_signal(
                    barrier, inc=1, device_id=(lax.rem(d + j, nd), peer[k], z),
                    device_id_type=MESH,
                )
                peers += 1
        for r in range(1, nz):
            pl.semaphore_signal(
                barrier, inc=1, device_id=(d, e, lax.rem(z + r, nz)), device_id_type=MESH
            )
            peers += 1
        for i in (5, 6, 0, 1, 4, 2, 3):
            loads[i].start()

        row = lax.broadcasted_iota(jnp.int32, (lanes, tokens), 0)
        group = row // CAP
        slot = row - group * CAP
        label = jnp.zeros((lanes, tokens), jnp.int32)
        for k in range(ne):
            label = jnp.where(group == k, peer[k], label)
        chosen = jnp.zeros((lanes, tokens), F32)
        scale = jnp.zeros((lanes, tokens), F32)
        loads[5].wait()
        loads[6].wait()
        for c in range(top):
            hit = routes[c : c + 1, :] == label
            chosen = chosen + jnp.where(hit, 1.0, 0.0)
            scale = scale + jnp.where(hit, combine[c : c + 1, :], 0.0)
        row_id = lax.broadcasted_iota(jnp.int32, (tokens, tokens), 0)
        col_id = lax.broadcasted_iota(jnp.int32, (tokens, tokens), 1)
        upper = jnp.where(row_id < col_id, 1.0, 0.0).astype(BF16)
        before = dot(chosen.astype(BF16), upper, 1, 0)
        keep = jnp.logical_and(chosen > 0.0, before == slot.astype(F32))
        pick_f = jnp.where(keep, 1.0, 0.0)
        pick = pick_f.astype(BF16)
        factor = jnp.sum(pick_f * scale, axis=1, keepdims=True)
        pick_ref[...] = pick

        loads[0].wait()
        loads[1].wait()

        def dispatch(k, j, c):
            lo, hi = pick_cuts[c]
            span = pl.ds(lo, hi - lo)
            return pltpu.make_async_remote_copy(
                src_ref=send.at[k, j, :, span], dst_ref=recv.at[k, d, :, span],
                send_sem=d_send.at[k, j, c], recv_sem=d_recv.at[k, d, c],
                device_id=(lax.rem(d + j, nd), peer[k], z), device_id_type=MESH,
            )

        for j in range(nd - 1, -1, -1):
            dj = lax.rem(d + j, nd)
            for lo, hi in pick_cuts:
                span = pl.ds(pl.multiple_of(dj * half + lo, 128), hi - lo)
                in_pick = dot(pick, li[:, span], 1, 0)
                gr_pick = dot(pick, go[:, span], 1, 0) * factor
                for k in range(ne):
                    at = k * CAP
                    tile = jnp.concatenate(
                        [in_pick[at : at + CAP], gr_pick[at : at + CAP]], axis=0
                    ).astype(BF16)
                    if j == 0 and k == 0:
                        recv[0, d, :, lo:hi] = tile
                    else:
                        send[k, j, :, lo:hi] = tile
        pl.semaphore_wait(barrier, peers)
        def send_rows(ks):
            for k in ks:
                for j in range(nd - 1, -1, -1):
                    if j or k:
                        for c in range(len(pick_cuts)):
                            dispatch(k, j, c).start()

        far = range(groups[last][0], ne)
        send_rows([*range(1, far[0]), 0])
        loads[4].wait()
        dw_t[...] = dw[...].T
        loads[2].wait()
        loads[3].wait()

        def arrived(k, s):
            for c, (lo, hi) in enumerate(pick_cuts):
                ref = recv.at[k, s, :, pl.ds(lo, hi - lo)]
                pltpu.make_async_copy(ref, ref, d_recv.at[k, s, c]).wait()

        def take(v, which):
            n = v.shape[0] // (2 * CAP)
            return v.reshape(n, 2, CAP, hidden)[:, which].reshape(n * CAP, hidden)

        def exchange(g, j):
            lo, hi = (k * nd * CAP for k in groups[g])
            span = pl.ds(lo, hi - lo)
            return pltpu.make_async_remote_copy(
                src_ref=psend.at[:, span], dst_ref=precv.at[j - 1, :, span],
                send_sem=p_send.at[g, j - 1], recv_sem=p_recv.at[g, j - 1],
                device_id=(lax.rem(d + j, nd), e, z), device_id_type=MESH,
            )

        def project(g):
            k0, k1 = groups[g]
            for k in range(k0, k1):
                if k == 0:
                    for j in range(1, nd):
                        arrived(0, lax.rem(d + j, nd))
                else:
                    for s in range(nd):
                        arrived(k, s)
            x = recv[k0:k1].reshape((k1 - k0) * nd * 2 * CAP, half)
            sums = [
                take(dot(x, gw[...], 1, 0), 0),
                take(dot(x, uw[...], 1, 0), 0),
                take(dot(x, dw_t[...], 1, 0), 1),
            ]
            lo, hi = k0 * nd * CAP, k1 * nd * CAP
            for i, v in enumerate(sums):
                psend[i, lo:hi] = v.astype(BF16)
            for j in range(1, nd):
                exchange(g, j).start()
            return sums

        def term_copy(k, s, c):
            lo, hi = back_cuts[c]
            span = pl.ds(lo, hi - lo)
            return pltpu.make_async_remote_copy(
                src_ref=rowg.at[k, s, :, span], dst_ref=terms.at[z, k, :, span],
                send_sem=r_send.at[k, s, c], recv_sem=r_recv.at[z, k, c],
                device_id=(s, peer[k], nd * s + d), device_id_type=MESH,
            )

        def own_copy(s, c):
            lo, hi = back_cuts[c]
            span = pl.ds(lo, hi - lo)
            return pltpu.make_async_copy(
                rowg.at[0, s, :, span], terms.at[z, 0, :, span], r_recv.at[z, 0, c]
            )

        def is_own(s):
            return jnp.logical_and(d == s, z == nd * s + d)

        def finish(g, sums):
            k0, k1 = groups[g]
            lo, hi = k0 * nd * CAP, k1 * nd * CAP
            gate, up, dhid = sums
            for j in range(1, nd):
                exchange(g, j).wait_recv()
                gate = gate + precv[j - 1, 0, lo:hi].astype(F32)
                up = up + precv[j - 1, 1, lo:hi].astype(F32)
                dhid = dhid + precv[j - 1, 2, lo:hi].astype(F32)
            sigma = jax.nn.sigmoid(gate)
            silu = gate * sigma
            act = silu * up
            d_up = dhid * silu
            d_gate = dhid * up * sigma * (1.0 + gate * (1.0 - sigma))
            both = jnp.concatenate([d_gate.astype(BF16), d_up.astype(BF16)], axis=1)
            for c, (at, to) in enumerate(back_cuts):
                grad = dot(both, back_t[:, at:to], 1, 0)
                grad = grad.reshape(k1 - k0, nd, CAP, to - at).astype(BF16)
                for k in range(k0, k1):
                    for s in range(nd):
                        rowg[k, s, :, at:to] = grad[k - k0, s]
                        if k:
                            term_copy(k, s, c).start()
                            continue

                        @pl.when(is_own(s))
                        def _():
                            own_copy(s, c).start()

                        @pl.when(jnp.logical_not(is_own(s)))
                        def _():
                            term_copy(0, s, c).start()
            for i, v in enumerate((d_gate, d_up, act)):
                v = v.reshape((k1 - k0) * nd, CAP, hidden)
                zero = jnp.zeros_like(v)
                pair = [zero, v] if i == 2 else [v, zero]
                pads[i, k0 * nd : k1 * nd] = jnp.concatenate(pair, axis=1).astype(BF16)

        def gather(g, r, c):
            k0, k1 = groups[g]
            lo, hi = back_cuts[c]
            ref = agbuf.at[part, pl.ds(k0, k1 - k0), :, pl.ds(lo, hi - lo)]
            return pltpu.make_async_remote_copy(
                src_ref=ref, dst_ref=ref,
                send_sem=a_send.at[g, r - 1, c], recv_sem=a_recv.at[g, part, c],
                device_id=(d, e, lax.rem(z + r, nz)), device_id_type=MESH,
            )

        def reduce(g):
            k0, k1 = groups[g]

            @pl.when(reducer)
            def _():
                for c, (lo, hi) in enumerate(back_cuts):
                    for k in range(k0, k1):
                        for q in range(nz):
                            ref = terms.at[q, k, :, pl.ds(lo, hi - lo)]
                            pltpu.make_async_copy(ref, ref, r_recv.at[q, k, c]).wait()
                    total = terms[0, k0:k1, :, lo:hi].astype(F32)
                    for q in range(1, nz):
                        total = total + terms[q, k0:k1, :, lo:hi].astype(F32)
                    agbuf[part, k0:k1, :, lo:hi] = total.astype(BF16)
                    for r in range(1, nz):
                        gather(g, r, c).start()

        every = ne * nd * 2 * CAP

        def weight_grad(i):
            x = recv[...].reshape(every, half)
            v = pads[i].reshape(every, hidden)
            if i == 2:
                gd_ref[0] = (dot(v, x, 0, 0) * 0.25).astype(BF16)
            else:
                (gg_ref, gu_ref)[i][0] = (dot(x, v, 0, 0) * 0.25).astype(BF16)

        for g in range(len(groups)):
            sums = project(g)
            if g == 0:
                back_t[:hidden] = gw[...].T
                back_t[hidden:] = uw[...].T
                send_rows(far)
            if g == last:
                for h in range(last - 1):
                    reduce(h)
            finish(g, sums)
        for i in range(3):
            weight_grad(i)
        for h in range(max(last - 1, 0), last + 1):
            reduce(h)

        for g, (k0, k1) in enumerate(groups):
            for c, (lo, hi) in enumerate(back_cuts):
                for h in range(nd):
                    @pl.when(part != h)
                    def _():
                        ref = agbuf.at[h, pl.ds(k0, k1 - k0), :, pl.ds(lo, hi - lo)]
                        pltpu.make_async_copy(ref, ref, a_recv.at[g, h, c]).wait()

        for k in range(ne):
            for j in range(nd):
                if j or k:
                    for c in range(len(pick_cuts)):
                        dispatch(k, j, c).wait_send()
        for g in range(len(groups)):
            for j in range(1, nd):
                exchange(g, j).wait_send()
        for c in range(len(back_cuts)):
            for k in range(ne):
                for s in range(nd):
                    if k:
                        term_copy(k, s, c).wait_send()
                    else:
                        @pl.when(jnp.logical_not(is_own(s)))
                        def _():
                            term_copy(0, s, c).wait_send()

        @pl.when(reducer)
        def _():
            for g in range(len(groups)):
                for c in range(len(back_cuts)):
                    for r in range(1, nz):
                        gather(g, r, c).wait_send()

    return kernel


def make_store(nd, lanes, half):
    parts = [(h, lo, hi) for h in range(nd) for lo, hi in cuts(half, STORE_PARTS // nd)]

    def kernel(agbuf, pick_ref, gg, gu, gd, out, gg_out, gu_out, gd_out, out_v, sem, out_sem):
        copies = [
            pltpu.make_async_copy(src, dst, sem.at[i])
            for i, (src, dst) in enumerate(((gg, gg_out), (gu, gu_out), (gd, gd_out)))
        ]
        for c in copies:
            c.start()
        pick = pick_ref[...]
        for i, (h, lo, hi) in enumerate(parts):
            got = agbuf[h, :, :, lo:hi].astype(F32).reshape(lanes, hi - lo).astype(BF16)
            span = pl.ds(h * half + lo, hi - lo)
            out_v[:, span] = dot(pick, got, 0, 0).astype(BF16)
            c = pltpu.make_async_copy(out_v.at[:, span], out.at[:, span], out_sem.at[i])
            c.start()
            copies.append(c)
        for c in copies:
            c.wait()

    return kernel, len(parts)


def body(grad_out, layer_in, routes, combine, gate_weight, up_weight, down_weight):
    nd = lax.axis_size("dp")
    ne = lax.axis_size("expert")
    nz = lax.axis_size("tensor")
    tokens, width = grad_out.shape
    top = routes.shape[1]
    half, hidden = gate_weight.shape[1:]
    lanes = ne * CAP
    groups = len(group_ranges(ne))
    kernel = make_kernel(nd, ne, nz, tokens, width, half, hidden, top)
    hbm = pl.BlockSpec(memory_space=pltpu.HBM)
    vmem = pl.BlockSpec(memory_space=pltpu.VMEM)
    dma = pltpu.SemaphoreType.DMA
    held = 2 * (nd * lanes * half + lanes * tokens + 3 * half * hidden)
    room = VMEM - held
    arrays = pl.pallas_call(
        kernel,
        out_shape=(
            pltpu.VMEM((nd, ne, CAP, half), BF16),
            pltpu.VMEM((lanes, tokens), BF16),
            pltpu.VMEM(gate_weight.shape, BF16),
            pltpu.VMEM(up_weight.shape, BF16),
            pltpu.VMEM(down_weight.shape, BF16),
        ),
        in_specs=[hbm] * 7,
        out_specs=(vmem,) * 5,
        scratch_shapes=[
            pltpu.VMEM((tokens, width), BF16),
            pltpu.VMEM((tokens, width), BF16),
            pltpu.VMEM((top, tokens), jnp.int32),
            pltpu.VMEM((top, tokens), F32),
            pltpu.VMEM((half, hidden), BF16),
            pltpu.VMEM((half, hidden), BF16),
            pltpu.VMEM((hidden, half), BF16),
            pltpu.VMEM((half, hidden), BF16),
            pltpu.VMEM((2 * hidden, half), BF16),
            pltpu.VMEM((ne, nd, 2 * CAP, half), BF16),
            pltpu.VMEM((ne, nd, 2 * CAP, half), BF16),
            pltpu.VMEM((3, ne * nd * CAP, hidden), BF16),
            pltpu.VMEM((nd - 1, 3, ne * nd * CAP, hidden), BF16),
            pltpu.VMEM((ne, nd, CAP, half), BF16),
            pltpu.VMEM((nz, ne, CAP, half), BF16),
            pltpu.VMEM((3, ne * nd, 2 * CAP, hidden), BF16),
            dma((7,)),
            dma((ne, nd, PICK_PARTS)),
            dma((ne, nd, PICK_PARTS)),
            dma((groups, nd - 1)),
            dma((groups, nd - 1)),
            dma((ne, nd, BACK_PARTS)),
            dma((nz, ne, BACK_PARTS)),
            dma((groups, nz - 1, BACK_PARTS)),
            dma((groups, nd, BACK_PARTS)),
        ],
        compiler_params=pltpu.CompilerParams(
            collective_id=0, has_side_effects=True, vmem_limit_bytes=room
        ),
    )(grad_out, layer_in, routes.T, combine.T, gate_weight, up_weight, down_weight)
    store, parts = make_store(nd, lanes, half)
    return tuple(pl.pallas_call(
        store,
        out_shape=tuple(
            jax.ShapeDtypeStruct(v.shape, BF16)
            for v in (grad_out, gate_weight, up_weight, down_weight)
        ),
        in_specs=[vmem] * 5,
        out_specs=(hbm,) * 4,
        scratch_shapes=[pltpu.VMEM((tokens, width), BF16), dma((3,)), dma((parts,))],
        compiler_params=pltpu.CompilerParams(vmem_limit_bytes=16 * 2**20),
    )(*[pltpu.with_memory_space_constraint(a, pltpu.VMEM) for a in arrays]))


def solution(mesh):
    return jax.shard_map(
        body,
        mesh=mesh,
        in_specs=(
            P(("dp", "expert"), None),
            P(("dp", "expert"), None),
            P(("dp", "expert"), None),
            P(("dp", "expert"), None),
            P("expert", "dp", "tensor"),
            P("expert", "dp", "tensor"),
            P("expert", "tensor", "dp"),
        ),
        out_specs=(
            P(("dp", "expert"), None),
            P("expert", "dp", "tensor"),
            P("expert", "dp", "tensor"),
            P("expert", "tensor", "dp"),
        ),
        check_vma=False,
    )
```

```python
import jax
import jax.numpy as jnp
from jax import lax
from jax.experimental import pallas as pl
from jax.experimental.pallas import tpu as pltpu
from jax.sharding import PartitionSpec as P

CAP = 8
BACK_PARTS = 2
STORE_PARTS = 4
VMEM = 67043328
MESH = pl.DeviceIdType.MESH
F32 = jnp.float32
BF16 = jnp.bfloat16


def dot(a, b, ca, cb):
    return lax.dot_general(a, b, (((ca,), (cb,)), ((), ())), preferred_element_type=F32)


def cuts(extent, parts):
    tiles = extent // 128
    edges = [128 * ((tiles * c + parts - 1) // parts) for c in range(parts + 1)]
    return list(zip(edges[:-1], edges[1:]))


def partner(e, k, ne):
    out, bit = 0, 1
    while bit < ne:
        own = lax.rem(lax.div(e, bit), 2)
        out = out + bit * ((1 - own) if k & bit else own)
        bit *= 2
    return out


def group_ranges(ne):
    edges = sorted({0, 1, 3 * ne // 4, ne})
    return list(zip(edges[:-1], edges[1:]))


def make_kernel(nd, ne, nz, tokens, width, half, hidden, top):
    lanes = ne * CAP
    groups = group_ranges(ne)
    last = len(groups) - 1
    group_of = [g for g, (k0, k1) in enumerate(groups) for _ in range(k0, k1)]
    back_cuts = cuts(half, BACK_PARTS)

    def kernel(
        go_hbm, li_hbm, routes_hbm, combine_hbm, gw_hbm, uw_hbm, dw_hbm,
        agbuf, pick_ref, gg_ref, gu_ref, gd_ref,
        tok, routes, combine, w2, dw, dw_t, back_t, send, recv, psend, precv, rowg, terms, pads,
        ld_sem, d_send, d_recv, p_send, p_recv, r_send, r_recv, a_send, a_recv,
    ):
        d = lax.axis_index("dp")
        e = lax.axis_index("expert")
        z = lax.axis_index("tensor")
        peer = [partner(e, k, ne) for k in range(ne)]
        part = z - (nd * d)
        reducer = jnp.logical_and(part >= 0, part < nd)

        loads = [
            pltpu.make_async_copy(routes_hbm, routes, ld_sem.at[0]),
            pltpu.make_async_copy(combine_hbm, combine, ld_sem.at[1]),
            pltpu.make_async_copy(li_hbm, tok.at[0], ld_sem.at[2]),
            pltpu.make_async_copy(go_hbm, tok.at[1], ld_sem.at[2]),
            pltpu.make_async_copy(dw_hbm.at[0], dw, ld_sem.at[3]),
            pltpu.make_async_copy(gw_hbm.at[0], w2.at[0], ld_sem.at[4]),
            pltpu.make_async_copy(uw_hbm.at[0], w2.at[1], ld_sem.at[4]),
        ]

        def settle(ref, sem):
            pltpu.make_async_copy(ref, ref, sem).wait()

        barrier = pltpu.get_barrier_semaphore()
        peers = 0
        for k in range(ne - 1, -1, -1):
            for j in range(nd):
                if j == 0 and k == 0:
                    continue
                pl.semaphore_signal(
                    barrier, inc=1, device_id=(lax.rem(d + j, nd), peer[k], z),
                    device_id_type=MESH,
                )
                peers += 1
        for r in range(1, nz):
            pl.semaphore_signal(
                barrier, inc=1, device_id=(d, e, lax.rem(z + r, nz)), device_id_type=MESH
            )
            peers += 1
        for c in loads:
            c.start()

        row = lax.broadcasted_iota(jnp.int32, (lanes, tokens), 0)
        group = row // CAP
        slot = row - group * CAP
        label = jnp.zeros((lanes, tokens), jnp.int32)
        for k in range(ne):
            label = jnp.where(group == k, peer[k], label)
        chosen = jnp.zeros((lanes, tokens), F32)
        scale = jnp.zeros((lanes, tokens), F32)
        settle(routes, ld_sem.at[0])
        settle(combine, ld_sem.at[1])
        for c in range(top):
            hit = routes[c : c + 1, :] == label
            chosen = chosen + jnp.where(hit, 1.0, 0.0)
            scale = scale + jnp.where(hit, combine[c : c + 1, :], 0.0)
        row_id = lax.broadcasted_iota(jnp.int32, (tokens, tokens), 0)
        col_id = lax.broadcasted_iota(jnp.int32, (tokens, tokens), 1)
        upper = jnp.where(row_id < col_id, 1.0, 0.0).astype(BF16)
        before = dot(chosen.astype(BF16), upper, 1, 0)
        keep = jnp.logical_and(chosen > 0.0, before == slot.astype(F32))
        pick_f = jnp.where(keep, 1.0, 0.0)
        pick = pick_f.astype(BF16)
        factor = jnp.sum(pick_f * scale, axis=1, keepdims=True)
        pick_ref[...] = pick

        settle(tok, ld_sem.at[2])

        def dispatch(k, j):
            return pltpu.make_async_remote_copy(
                src_ref=send.at[k * nd + j - 1], dst_ref=recv.at[k, d],
                send_sem=d_send.at[0], recv_sem=d_recv.at[group_of[k]],
                device_id=(lax.rem(d + j, nd), peer[k], z), device_id_type=MESH,
            )

        for j in range(nd - 1, -1, -1):
            dj = lax.rem(d + j, nd)
            span = pl.ds(pl.multiple_of(dj * half, 128), half)
            in_pick = dot(pick, tok[0, :, span], 1, 0)
            gr_pick = dot(pick, tok[1, :, span], 1, 0) * factor
            for k in range(ne):
                at = k * CAP
                tile = jnp.concatenate(
                    [in_pick[at : at + CAP], gr_pick[at : at + CAP]], axis=0
                ).astype(BF16)
                if j == 0 and k == 0:
                    recv[0, d] = tile
                else:
                    send[k * nd + j - 1] = tile
        pl.semaphore_wait(barrier, peers)
        def send_rows(ks):
            for k in ks:
                for j in range(nd - 1, -1, -1):
                    if j or k:
                        dispatch(k, j).start()

        far = range(groups[last][0], ne)
        send_rows([*range(1, far[0]), 0])
        settle(dw, ld_sem.at[3])
        dw_t[...] = dw[...].T
        settle(w2, ld_sem.at[4])

        def take(v, which):
            n = v.shape[0] // (2 * CAP)
            return v.reshape(n, 2, CAP, hidden)[:, which].reshape(n * CAP, hidden)

        def exchange(g, j):
            lo, hi = (k * nd * CAP for k in groups[g])
            span = pl.ds(lo, hi - lo)
            return pltpu.make_async_remote_copy(
                src_ref=psend.at[:, span], dst_ref=precv.at[j - 1, :, span],
                send_sem=p_send.at[0], recv_sem=p_recv.at[g],
                device_id=(lax.rem(d + j, nd), e, z), device_id_type=MESH,
            )

        def project(g):
            k0, k1 = groups[g]
            if g:
                settle(recv.at[pl.ds(k0, k1 - k0)], d_recv.at[g])
            else:
                for j in range(1, nd):
                    settle(recv.at[0, lax.rem(d + j, nd)], d_recv.at[0])
            x = recv[k0:k1].reshape((k1 - k0) * nd * 2 * CAP, half)
            sums = [
                take(dot(x, w2[0], 1, 0), 0),
                take(dot(x, w2[1], 1, 0), 0),
                take(dot(x, dw_t[...], 1, 0), 1),
            ]
            lo, hi = k0 * nd * CAP, k1 * nd * CAP
            for i, v in enumerate(sums):
                psend[i, lo:hi] = v.astype(BF16)
            for j in range(1, nd):
                exchange(g, j).start()
            return sums

        def term_copy(k, s, c):
            lo, hi = back_cuts[c]
            span = pl.ds(lo, hi - lo)
            return pltpu.make_async_remote_copy(
                src_ref=rowg.at[k, s, :, span], dst_ref=terms.at[z, k, :, span],
                send_sem=r_send.at[nd if k else s], recv_sem=r_recv.at[group_of[k], c],
                device_id=(s, peer[k], nd * s + d), device_id_type=MESH,
            )

        def own_copy(s, c):
            lo, hi = back_cuts[c]
            span = pl.ds(lo, hi - lo)
            return pltpu.make_async_copy(
                rowg.at[0, s, :, span], terms.at[z, 0, :, span], r_recv.at[0, c]
            )

        def is_own(s):
            return jnp.logical_and(d == s, z == nd * s + d)

        def finish(g, sums):
            k0, k1 = groups[g]
            lo, hi = k0 * nd * CAP, k1 * nd * CAP
            gate, up, dhid = sums
            settle(precv.at[:, :, pl.ds(lo, hi - lo)], p_recv.at[g])
            for j in range(1, nd):
                gate = gate + precv[j - 1, 0, lo:hi].astype(F32)
                up = up + precv[j - 1, 1, lo:hi].astype(F32)
                dhid = dhid + precv[j - 1, 2, lo:hi].astype(F32)
            sigma = jax.nn.sigmoid(gate)
            silu = gate * sigma
            act = silu * up
            d_up = dhid * silu
            d_gate = dhid * up * sigma * (1.0 + gate * (1.0 - sigma))
            both = jnp.concatenate([d_gate.astype(BF16), d_up.astype(BF16)], axis=1)
            for c, (at, to) in enumerate(back_cuts):
                grad = dot(both, back_t[:, at:to], 1, 0)
                grad = grad.reshape(k1 - k0, nd, CAP, to - at).astype(BF16)
                for k in range(k0, k1):
                    for s in range(nd):
                        rowg[k, s, :, at:to] = grad[k - k0, s]
                        if k:
                            term_copy(k, s, c).start()
                            continue

                        @pl.when(is_own(s))
                        def _():
                            own_copy(s, c).start()

                        @pl.when(jnp.logical_not(is_own(s)))
                        def _():
                            term_copy(0, s, c).start()
            for i, v in enumerate((d_gate, d_up, act)):
                v = v.reshape((k1 - k0) * nd, CAP, hidden)
                zero = jnp.zeros_like(v)
                pair = [zero, v] if i == 2 else [v, zero]
                pads[i, k0 * nd : k1 * nd] = jnp.concatenate(pair, axis=1).astype(BF16)

        def gather(g, r, c):
            k0, k1 = groups[g]
            lo, hi = back_cuts[c]
            ref = agbuf.at[part, pl.ds(k0, k1 - k0), :, pl.ds(lo, hi - lo)]
            return pltpu.make_async_remote_copy(
                src_ref=ref, dst_ref=ref,
                send_sem=a_send.at[0], recv_sem=a_recv.at[0],
                device_id=(d, e, lax.rem(z + r, nz)), device_id_type=MESH,
            )

        def reduce(g):
            k0, k1 = groups[g]

            @pl.when(reducer)
            def _():
                for c, (lo, hi) in enumerate(back_cuts):
                    settle(terms.at[:, pl.ds(k0, k1 - k0), :, pl.ds(lo, hi - lo)], r_recv.at[g, c])
                    total = terms[0, k0:k1, :, lo:hi].astype(F32)
                    for q in range(1, nz):
                        total = total + terms[q, k0:k1, :, lo:hi].astype(F32)
                    agbuf[part, k0:k1, :, lo:hi] = total.astype(BF16)
                    for r in range(1, nz):
                        gather(g, r, c).start()

        every = ne * nd * 2 * CAP

        def weight_grad(i):
            x = recv[...].reshape(every, half)
            v = pads[i].reshape(every, hidden)
            if i == 2:
                gd_ref[0] = (dot(v, x, 0, 0) * 0.25).astype(BF16)
            else:
                (gg_ref, gu_ref)[i][0] = (dot(x, v, 0, 0) * 0.25).astype(BF16)

        for g in range(len(groups)):
            sums = project(g)
            if g == 0:
                back_t[:hidden] = w2[0].T
                back_t[hidden:] = w2[1].T
                send_rows(far)
            if g == last:
                for h in range(last - 1):
                    reduce(h)
            finish(g, sums)
        for i in range(3):
            weight_grad(i)
        settle(send, d_send.at[0])
        settle(precv, p_send.at[0])
        settle(rowg.at[pl.ds(1, ne - 1)], r_send.at[nd])
        for s in range(nd):
            @pl.when(jnp.logical_not(is_own(s)))
            def _():
                settle(rowg.at[0, s], r_send.at[s])

        for h in range(max(last - 1, 0), last + 1):
            reduce(h)

        @pl.when(jnp.logical_not(reducer))
        def _():
            settle(agbuf, a_recv.at[0])

        @pl.when(reducer)
        def _():
            settle(agbuf.at[pl.ds(0, nd - 1)], a_recv.at[0])
            settle(terms.at[pl.ds(0, nz - 1)], a_send.at[0])

    return kernel


def make_store(nd, lanes, half):
    parts = [(h, lo, hi) for h in range(nd) for lo, hi in cuts(half, STORE_PARTS // nd)]

    def kernel(agbuf, pick_ref, gg, gu, gd, out, gg_out, gu_out, gd_out, out_v, sem, out_sem):
        copies = [
            pltpu.make_async_copy(src, dst, sem.at[i])
            for i, (src, dst) in enumerate(((gg, gg_out), (gu, gu_out), (gd, gd_out)))
        ]
        for c in copies:
            c.start()
        pick = pick_ref[...]
        for i, (h, lo, hi) in enumerate(parts):
            got = agbuf[h, :, :, lo:hi].astype(F32).reshape(lanes, hi - lo).astype(BF16)
            span = pl.ds(h * half + lo, hi - lo)
            out_v[:, span] = dot(pick, got, 0, 0).astype(BF16)
            c = pltpu.make_async_copy(out_v.at[:, span], out.at[:, span], out_sem.at[i])
            c.start()
            copies.append(c)
        for c in copies:
            c.wait()

    return kernel, len(parts)


def body(grad_out, layer_in, routes, combine, gate_weight, up_weight, down_weight):
    nd = lax.axis_size("dp")
    ne = lax.axis_size("expert")
    nz = lax.axis_size("tensor")
    tokens, width = grad_out.shape
    top = routes.shape[1]
    half, hidden = gate_weight.shape[1:]
    lanes = ne * CAP
    groups = len(group_ranges(ne))
    kernel = make_kernel(nd, ne, nz, tokens, width, half, hidden, top)
    hbm = pl.BlockSpec(memory_space=pltpu.HBM)
    vmem = pl.BlockSpec(memory_space=pltpu.VMEM)
    dma = pltpu.SemaphoreType.DMA
    held = 2 * (nd * lanes * half + lanes * tokens + 3 * half * hidden)
    room = VMEM - held
    arrays = pl.pallas_call(
        kernel,
        out_shape=(
            pltpu.VMEM((nd, ne, CAP, half), BF16),
            pltpu.VMEM((lanes, tokens), BF16),
            pltpu.VMEM(gate_weight.shape, BF16),
            pltpu.VMEM(up_weight.shape, BF16),
            pltpu.VMEM(down_weight.shape, BF16),
        ),
        in_specs=[hbm] * 7,
        out_specs=(vmem,) * 5,
        scratch_shapes=[
            pltpu.VMEM((2, tokens, width), BF16),
            pltpu.VMEM((top, tokens), jnp.int32),
            pltpu.VMEM((top, tokens), F32),
            pltpu.VMEM((2, half, hidden), BF16),
            pltpu.VMEM((hidden, half), BF16),
            pltpu.VMEM((half, hidden), BF16),
            pltpu.VMEM((2 * hidden, half), BF16),
            pltpu.VMEM((ne * nd - 1, 2 * CAP, half), BF16),
            pltpu.VMEM((ne, nd, 2 * CAP, half), BF16),
            pltpu.VMEM((3, ne * nd * CAP, hidden), BF16),
            pltpu.VMEM((nd - 1, 3, ne * nd * CAP, hidden), BF16),
            pltpu.VMEM((ne, nd, CAP, half), BF16),
            pltpu.VMEM((nz, ne, CAP, half), BF16),
            pltpu.VMEM((3, ne * nd, 2 * CAP, hidden), BF16),
            dma((5,)),
            dma((1,)),
            dma((groups,)),
            dma((1,)),
            dma((groups,)),
            dma((nd + 1,)),
            dma((groups, BACK_PARTS)),
            dma((1,)),
            dma((1,)),
        ],
        compiler_params=pltpu.CompilerParams(
            collective_id=0, has_side_effects=True, vmem_limit_bytes=room
        ),
    )(grad_out, layer_in, routes.T, combine.T, gate_weight, up_weight, down_weight)
    store, parts = make_store(nd, lanes, half)
    return tuple(pl.pallas_call(
        store,
        out_shape=tuple(
            jax.ShapeDtypeStruct(v.shape, BF16)
            for v in (grad_out, gate_weight, up_weight, down_weight)
        ),
        in_specs=[vmem] * 5,
        out_specs=(hbm,) * 4,
        scratch_shapes=[pltpu.VMEM((tokens, width), BF16), dma((3,)), dma((parts,))],
        compiler_params=pltpu.CompilerParams(vmem_limit_bytes=16 * 2**20),
    )(*[pltpu.with_memory_space_constraint(a, pltpu.VMEM) for a in arrays]))


def solution(mesh):
    return jax.shard_map(
        body,
        mesh=mesh,
        in_specs=(
            P(("dp", "expert"), None),
            P(("dp", "expert"), None),
            P(("dp", "expert"), None),
            P(("dp", "expert"), None),
            P("expert", "dp", "tensor"),
            P("expert", "dp", "tensor"),
            P("expert", "tensor", "dp"),
        ),
        out_specs=(
            P(("dp", "expert"), None),
            P("expert", "dp", "tensor"),
            P("expert", "dp", "tensor"),
            P("expert", "tensor", "dp"),
        ),
        check_vma=False,
    )
```

```python
import jax
import jax.numpy as jnp
from jax import lax
from jax.experimental import pallas as pl
from jax.experimental.pallas import tpu as pltpu
from jax.sharding import PartitionSpec as P

CAP = 8
BACK_PARTS = (1, 2, 2)
FAR_PARTS = 2
STORE_PARTS = 4
VMEM = 67043328
MESH = pl.DeviceIdType.MESH
F32 = jnp.float32
BF16 = jnp.bfloat16


def dot(a, b, ca, cb):
    return lax.dot_general(a, b, (((ca,), (cb,)), ((), ())), preferred_element_type=F32)


def cuts(extent, parts):
    tiles = extent // 128
    edges = [128 * ((tiles * c + parts - 1) // parts) for c in range(parts + 1)]
    return list(zip(edges[:-1], edges[1:]))


def partner(e, k, ne):
    out, bit = 0, 1
    while bit < ne:
        own = lax.rem(lax.div(e, bit), 2)
        out = out + bit * ((1 - own) if k & bit else own)
        bit *= 2
    return out


def group_ranges(ne):
    edges = sorted({0, 1, 3 * ne // 4, ne})
    return list(zip(edges[:-1], edges[1:]))


def make_kernel(nd, ne, nz, tokens, width, half, hidden, top):
    lanes = ne * CAP
    groups = group_ranges(ne)
    last = len(groups) - 1
    group_of = [g for g, (k0, k1) in enumerate(groups) for _ in range(k0, k1)]
    back = [cuts(half, BACK_PARTS[min(g, 2)]) for g in range(len(groups))]
    sent = [cuts(half, FAR_PARTS if g == last else 1) for g in range(len(groups))]

    def kernel(
        go_hbm, li_hbm, routes_hbm, combine_hbm, gw_hbm, uw_hbm, dw_hbm,
        agbuf, pick_ref, gg_ref, gu_ref, gd_ref,
        tok, routes, combine, w2, dw, dw_t, back_t, send, recv, psend, precv, rowg, terms, pads,
        ld_sem, d_send, d_recv, p_send, p_recv, r_send, r_recv, a_send, a_recv,
    ):
        d = lax.axis_index("dp")
        e = lax.axis_index("expert")
        z = lax.axis_index("tensor")
        peer = [partner(e, k, ne) for k in range(ne)]
        part = z - (nd * d)
        reducer = jnp.logical_and(part >= 0, part < nd)

        loads = [
            pltpu.make_async_copy(routes_hbm, routes, ld_sem.at[0]),
            pltpu.make_async_copy(combine_hbm, combine, ld_sem.at[1]),
            pltpu.make_async_copy(li_hbm, tok.at[0], ld_sem.at[2]),
            pltpu.make_async_copy(go_hbm, tok.at[1], ld_sem.at[2]),
            pltpu.make_async_copy(dw_hbm.at[0], dw, ld_sem.at[3]),
            pltpu.make_async_copy(gw_hbm.at[0], w2.at[0], ld_sem.at[4]),
            pltpu.make_async_copy(uw_hbm.at[0], w2.at[1], ld_sem.at[4]),
        ]

        def settle(ref, sem):
            pltpu.make_async_copy(ref, ref, sem).wait()

        barrier = pltpu.get_barrier_semaphore()
        peers = 0
        for k in range(ne - 1, -1, -1):
            for j in range(nd):
                if j == 0 and k == 0:
                    continue
                pl.semaphore_signal(
                    barrier, inc=1, device_id=(lax.rem(d + j, nd), peer[k], z),
                    device_id_type=MESH,
                )
                peers += 1
        for r in range(1, nz):
            pl.semaphore_signal(
                barrier, inc=1, device_id=(d, e, lax.rem(z + r, nz)), device_id_type=MESH
            )
            peers += 1
        for c in loads:
            c.start()

        row = lax.broadcasted_iota(jnp.int32, (lanes, tokens), 0)
        group = row // CAP
        slot = row - group * CAP
        label = jnp.zeros((lanes, tokens), jnp.int32)
        for k in range(ne):
            label = jnp.where(group == k, peer[k], label)
        chosen = jnp.zeros((lanes, tokens), F32)
        scale = jnp.zeros((lanes, tokens), F32)
        settle(routes, ld_sem.at[0])
        settle(combine, ld_sem.at[1])
        for c in range(top):
            hit = routes[c : c + 1, :] == label
            chosen = chosen + jnp.where(hit, 1.0, 0.0)
            scale = scale + jnp.where(hit, combine[c : c + 1, :], 0.0)
        row_id = lax.broadcasted_iota(jnp.int32, (tokens, tokens), 0)
        col_id = lax.broadcasted_iota(jnp.int32, (tokens, tokens), 1)
        upper = jnp.where(row_id < col_id, 1.0, 0.0).astype(BF16)
        before = dot(chosen.astype(BF16), upper, 1, 0)
        keep = jnp.logical_and(chosen > 0.0, before == slot.astype(F32))
        pick_f = jnp.where(keep, 1.0, 0.0)
        pick = pick_f.astype(BF16)
        factor = jnp.sum(pick_f * scale, axis=1, keepdims=True)
        pick_ref[...] = pick

        settle(tok, ld_sem.at[2])

        def dispatch(k, j, c):
            lo, hi = sent[group_of[k]][c]
            span = pl.ds(lo, hi - lo)
            return pltpu.make_async_remote_copy(
                src_ref=send.at[k * nd + j - 1, :, span], dst_ref=recv.at[k, d, :, span],
                send_sem=d_send.at[0], recv_sem=d_recv.at[group_of[k], c],
                device_id=(lax.rem(d + j, nd), peer[k], z), device_id_type=MESH,
            )

        for j in range(nd - 1, -1, -1):
            dj = lax.rem(d + j, nd)
            span = pl.ds(pl.multiple_of(dj * half, 128), half)
            in_pick = dot(pick, tok[0, :, span], 1, 0)
            gr_pick = dot(pick, tok[1, :, span], 1, 0) * factor
            for k in range(ne):
                at = k * CAP
                tile = jnp.concatenate(
                    [in_pick[at : at + CAP], gr_pick[at : at + CAP]], axis=0
                ).astype(BF16)
                if j == 0 and k == 0:
                    recv[0, d] = tile
                else:
                    send[k * nd + j - 1] = tile
        pl.semaphore_wait(barrier, peers)
        def send_rows(ks):
            for k in ks:
                for c in range(len(sent[group_of[k]])):
                    for j in range(nd - 1, -1, -1):
                        if j or k:
                            dispatch(k, j, c).start()

        far = range(groups[last][0], ne)
        send_rows(range(far[0]))
        settle(dw, ld_sem.at[3])
        dw_t[...] = dw[...].T
        settle(w2, ld_sem.at[4])

        def take(v, which):
            n = v.shape[0] // (2 * CAP)
            return v.reshape(n, 2, CAP, hidden)[:, which].reshape(n * CAP, hidden)

        def exchange(g, j):
            lo, hi = (k * nd * CAP for k in groups[g])
            span = pl.ds(lo, hi - lo)
            return pltpu.make_async_remote_copy(
                src_ref=psend.at[:, span], dst_ref=precv.at[j - 1, :, span],
                send_sem=p_send.at[0], recv_sem=p_recv.at[g],
                device_id=(lax.rem(d + j, nd), e, z), device_id_type=MESH,
            )

        def project(g):
            k0, k1 = groups[g]
            rows = (k1 - k0) * nd * 2 * CAP
            sums = [jnp.zeros((rows, hidden), F32)] * 3
            for c, (lo, hi) in enumerate(sent[g]):
                span = pl.ds(lo, hi - lo)
                if g:
                    settle(recv.at[pl.ds(k0, k1 - k0), :, :, span], d_recv.at[g, c])
                else:
                    for j in range(1, nd):
                        settle(recv.at[0, lax.rem(d + j, nd), :, span], d_recv.at[0, c])
                x = recv[k0:k1, :, :, lo:hi].reshape(rows, hi - lo)
                for i, w in enumerate((w2.at[0], w2.at[1], dw_t)):
                    sums[i] = sums[i] + dot(x, w[lo:hi, :], 1, 0)
            sums = [take(v, i // 2) for i, v in enumerate(sums)]
            lo, hi = k0 * nd * CAP, k1 * nd * CAP
            for i, v in enumerate(sums):
                psend[i, lo:hi] = v.astype(BF16)
            for j in range(1, nd):
                exchange(g, j).start()
            return sums

        def term_copy(k, s, c):
            lo, hi = back[group_of[k]][c]
            span = pl.ds(lo, hi - lo)
            return pltpu.make_async_remote_copy(
                src_ref=rowg.at[k, s, :, span], dst_ref=terms.at[z, k, :, span],
                send_sem=r_send.at[nd if k else s], recv_sem=r_recv.at[group_of[k], c],
                device_id=(s, peer[k], nd * s + d), device_id_type=MESH,
            )

        def own_copy(s, c):
            lo, hi = back[0][c]
            span = pl.ds(lo, hi - lo)
            return pltpu.make_async_copy(
                rowg.at[0, s, :, span], terms.at[z, 0, :, span], r_recv.at[0, c]
            )

        def is_own(s):
            return jnp.logical_and(d == s, z == nd * s + d)

        def finish(g, sums):
            k0, k1 = groups[g]
            lo, hi = k0 * nd * CAP, k1 * nd * CAP
            gate, up, dhid = sums
            settle(precv.at[:, :, pl.ds(lo, hi - lo)], p_recv.at[g])
            for j in range(1, nd):
                gate = gate + precv[j - 1, 0, lo:hi].astype(F32)
                up = up + precv[j - 1, 1, lo:hi].astype(F32)
                dhid = dhid + precv[j - 1, 2, lo:hi].astype(F32)
            sigma = jax.nn.sigmoid(gate)
            silu = gate * sigma
            act = silu * up
            d_up = dhid * silu
            d_gate = dhid * up * sigma * (1.0 + gate * (1.0 - sigma))
            both = jnp.concatenate([d_gate.astype(BF16), d_up.astype(BF16)], axis=1)
            for c, (at, to) in enumerate(back[g]):
                grad = dot(both, back_t[:, at:to], 1, 0)
                grad = grad.reshape(k1 - k0, nd, CAP, to - at).astype(BF16)
                for k in range(k0, k1):
                    for s in range(nd):
                        rowg[k, s, :, at:to] = grad[k - k0, s]
                        if k:
                            term_copy(k, s, c).start()
                            continue

                        @pl.when(is_own(s))
                        def _():
                            own_copy(s, c).start()

                        @pl.when(jnp.logical_not(is_own(s)))
                        def _():
                            term_copy(0, s, c).start()
            for i, v in enumerate((d_gate, d_up, act)):
                v = v.reshape((k1 - k0) * nd, CAP, hidden)
                zero = jnp.zeros_like(v)
                pair = [zero, v] if i == 2 else [v, zero]
                pads[i, k0 * nd : k1 * nd] = jnp.concatenate(pair, axis=1).astype(BF16)

        def gather(g, r, c):
            k0, k1 = groups[g]
            lo, hi = back[g][c]
            ref = agbuf.at[part, pl.ds(k0, k1 - k0), :, pl.ds(lo, hi - lo)]
            return pltpu.make_async_remote_copy(
                src_ref=ref, dst_ref=ref,
                send_sem=a_send.at[0], recv_sem=a_recv.at[0],
                device_id=(d, e, lax.rem(z + r, nz)), device_id_type=MESH,
            )

        def reduce(g):
            k0, k1 = groups[g]

            @pl.when(reducer)
            def _():
                for c, (lo, hi) in enumerate(back[g]):
                    settle(terms.at[:, pl.ds(k0, k1 - k0), :, pl.ds(lo, hi - lo)], r_recv.at[g, c])
                    total = terms[0, k0:k1, :, lo:hi].astype(F32)
                    for q in range(1, nz):
                        total = total + terms[q, k0:k1, :, lo:hi].astype(F32)
                    agbuf[part, k0:k1, :, lo:hi] = total.astype(BF16)
                    for r in range(1, nz):
                        gather(g, r, c).start()

        every = ne * nd * 2 * CAP

        def weight_grad(i):
            x = recv[...].reshape(every, half)
            v = pads[i].reshape(every, hidden)
            if i == 2:
                gd_ref[0] = (dot(v, x, 0, 0) * 0.25).astype(BF16)
            else:
                (gg_ref, gu_ref)[i][0] = (dot(x, v, 0, 0) * 0.25).astype(BF16)

        for g in range(len(groups)):
            if g == last:
                for h in range(last - 1):
                    reduce(h)
            sums = project(g)
            if g == 0:
                back_t[:hidden] = w2[0].T
                back_t[hidden:] = w2[1].T
                send_rows(far)
            finish(g, sums)
        for i in range(3):
            weight_grad(i)
        settle(send, d_send.at[0])
        settle(precv, p_send.at[0])
        settle(rowg.at[pl.ds(1, ne - 1)], r_send.at[nd])
        for s in range(nd):
            @pl.when(jnp.logical_not(is_own(s)))
            def _():
                settle(rowg.at[0, s], r_send.at[s])

        for h in range(max(last - 1, 0), last + 1):
            reduce(h)

        @pl.when(jnp.logical_not(reducer))
        def _():
            settle(agbuf, a_recv.at[0])

        @pl.when(reducer)
        def _():
            settle(agbuf.at[pl.ds(0, nd - 1)], a_recv.at[0])
            settle(terms.at[pl.ds(0, nz - 1)], a_send.at[0])

    return kernel


def make_store(nd, lanes, half):
    parts = [(h, lo, hi) for h in range(nd) for lo, hi in cuts(half, STORE_PARTS // nd)]

    def kernel(agbuf, pick_ref, gg, gu, gd, out, gg_out, gu_out, gd_out, out_v, sem, out_sem):
        copies = [
            pltpu.make_async_copy(src, dst, sem.at[i])
            for i, (src, dst) in enumerate(((gg, gg_out), (gu, gu_out), (gd, gd_out)))
        ]
        for c in copies:
            c.start()
        pick = pick_ref[...]
        for i, (h, lo, hi) in enumerate(parts):
            got = agbuf[h, :, :, lo:hi].astype(F32).reshape(lanes, hi - lo).astype(BF16)
            span = pl.ds(h * half + lo, hi - lo)
            out_v[:, span] = dot(pick, got, 0, 0).astype(BF16)
            c = pltpu.make_async_copy(out_v.at[:, span], out.at[:, span], out_sem.at[i])
            c.start()
            copies.append(c)
        for c in copies:
            c.wait()

    return kernel, len(parts)


def body(grad_out, layer_in, routes, combine, gate_weight, up_weight, down_weight):
    nd = lax.axis_size("dp")
    ne = lax.axis_size("expert")
    nz = lax.axis_size("tensor")
    tokens, width = grad_out.shape
    top = routes.shape[1]
    half, hidden = gate_weight.shape[1:]
    lanes = ne * CAP
    groups = len(group_ranges(ne))
    kernel = make_kernel(nd, ne, nz, tokens, width, half, hidden, top)
    hbm = pl.BlockSpec(memory_space=pltpu.HBM)
    vmem = pl.BlockSpec(memory_space=pltpu.VMEM)
    dma = pltpu.SemaphoreType.DMA
    held = 2 * (nd * lanes * half + lanes * tokens + 3 * half * hidden)
    room = VMEM - held
    arrays = pl.pallas_call(
        kernel,
        out_shape=(
            pltpu.VMEM((nd, ne, CAP, half), BF16),
            pltpu.VMEM((lanes, tokens), BF16),
            pltpu.VMEM(gate_weight.shape, BF16),
            pltpu.VMEM(up_weight.shape, BF16),
            pltpu.VMEM(down_weight.shape, BF16),
        ),
        in_specs=[hbm] * 7,
        out_specs=(vmem,) * 5,
        scratch_shapes=[
            pltpu.VMEM((2, tokens, width), BF16),
            pltpu.VMEM((top, tokens), jnp.int32),
            pltpu.VMEM((top, tokens), F32),
            pltpu.VMEM((2, half, hidden), BF16),
            pltpu.VMEM((hidden, half), BF16),
            pltpu.VMEM((half, hidden), BF16),
            pltpu.VMEM((2 * hidden, half), BF16),
            pltpu.VMEM((ne * nd - 1, 2 * CAP, half), BF16),
            pltpu.VMEM((ne, nd, 2 * CAP, half), BF16),
            pltpu.VMEM((3, ne * nd * CAP, hidden), BF16),
            pltpu.VMEM((nd - 1, 3, ne * nd * CAP, hidden), BF16),
            pltpu.VMEM((ne, nd, CAP, half), BF16),
            pltpu.VMEM((nz, ne, CAP, half), BF16),
            pltpu.VMEM((3, ne * nd, 2 * CAP, hidden), BF16),
            dma((5,)),
            dma((1,)),
            dma((groups, FAR_PARTS)),
            dma((1,)),
            dma((groups,)),
            dma((nd + 1,)),
            dma((groups, max(BACK_PARTS))),
            dma((1,)),
            dma((1,)),
        ],
        compiler_params=pltpu.CompilerParams(
            collective_id=0, has_side_effects=True, vmem_limit_bytes=room
        ),
    )(grad_out, layer_in, routes.T, combine.T, gate_weight, up_weight, down_weight)
    store, parts = make_store(nd, lanes, half)
    return tuple(pl.pallas_call(
        store,
        out_shape=tuple(
            jax.ShapeDtypeStruct(v.shape, BF16)
            for v in (grad_out, gate_weight, up_weight, down_weight)
        ),
        in_specs=[vmem] * 5,
        out_specs=(hbm,) * 4,
        scratch_shapes=[pltpu.VMEM((tokens, width), BF16), dma((3,)), dma((parts,))],
        compiler_params=pltpu.CompilerParams(vmem_limit_bytes=16 * 2**20),
    )(*[pltpu.with_memory_space_constraint(a, pltpu.VMEM) for a in arrays]))


def solution(mesh):
    return jax.shard_map(
        body,
        mesh=mesh,
        in_specs=(
            P(("dp", "expert"), None),
            P(("dp", "expert"), None),
            P(("dp", "expert"), None),
            P(("dp", "expert"), None),
            P("expert", "dp", "tensor"),
            P("expert", "dp", "tensor"),
            P("expert", "tensor", "dp"),
        ),
        out_specs=(
            P(("dp", "expert"), None),
            P("expert", "dp", "tensor"),
            P("expert", "dp", "tensor"),
            P("expert", "tensor", "dp"),
        ),
        check_vma=False,
    )
```

```python
import jax
import jax.numpy as jnp
from jax import lax
from jax.experimental import pallas as pl
from jax.experimental.pallas import tpu as pltpu
from jax.sharding import PartitionSpec as P

CAP = 8
BACK_PARTS = (1, 2, 2)
FAR_PARTS = 2
STORE_PARTS = 4
VMEM = 67043328
MESH = pl.DeviceIdType.MESH
F32 = jnp.float32
BF16 = jnp.bfloat16


def dot(a, b, ca, cb):
    return lax.dot_general(a, b, (((ca,), (cb,)), ((), ())), preferred_element_type=F32)


def cuts(extent, parts):
    tiles = extent // 128
    edges = [128 * ((tiles * c + parts - 1) // parts) for c in range(parts + 1)]
    return list(zip(edges[:-1], edges[1:]))


def partner(e, k, ne):
    out, bit = 0, 1
    while bit < ne:
        own = lax.rem(lax.div(e, bit), 2)
        out = out + bit * ((1 - own) if k & bit else own)
        bit *= 2
    return out


def group_ranges(ne):
    edges = sorted({0, 1, 3 * ne // 4, ne})
    return list(zip(edges[:-1], edges[1:]))


def make_kernel(nd, ne, nz, tokens, width, half, hidden, top):
    lanes = ne * CAP
    groups = group_ranges(ne)
    last = len(groups) - 1
    group_of = [g for g, (k0, k1) in enumerate(groups) for _ in range(k0, k1)]
    back = [cuts(half, BACK_PARTS[min(g, 2)]) for g in range(len(groups))]
    sent = [cuts(half, FAR_PARTS if g == last else 1) for g in range(len(groups))]

    def kernel(
        go_hbm, li_hbm, routes_hbm, combine_hbm, gw_hbm, uw_hbm, dw_hbm,
        agbuf, pick_ref, gg_ref, gu_ref, gd_ref,
        tok, routes, combine, w2, dw, dw_t, back_t, send, recv, psend, precv, rowg, terms, pads,
        ld_sem, d_send, d_recv, p_send, p_recv, r_send, r_recv, a_send, a_recv,
    ):
        d = lax.axis_index("dp")
        e = lax.axis_index("expert")
        z = lax.axis_index("tensor")
        peer = [partner(e, k, ne) for k in range(ne)]
        part = z - (nd * d)
        reducer = jnp.logical_and(part >= 0, part < nd)

        loads = [
            pltpu.make_async_copy(routes_hbm, routes, ld_sem.at[0]),
            pltpu.make_async_copy(combine_hbm, combine, ld_sem.at[1]),
            pltpu.make_async_copy(li_hbm, tok.at[0], ld_sem.at[2]),
            pltpu.make_async_copy(go_hbm, tok.at[1], ld_sem.at[2]),
            pltpu.make_async_copy(dw_hbm.at[0], dw, ld_sem.at[3]),
            pltpu.make_async_copy(gw_hbm.at[0], w2.at[0], ld_sem.at[4]),
            pltpu.make_async_copy(uw_hbm.at[0], w2.at[1], ld_sem.at[4]),
        ]

        def settle(ref, sem):
            pltpu.make_async_copy(ref, ref, sem).wait()

        barrier = pltpu.get_barrier_semaphore()
        peers = 0
        for k in range(ne - 1, -1, -1):
            for j in range(nd):
                if j == 0 and k == 0:
                    continue
                pl.semaphore_signal(
                    barrier, inc=1, device_id=(lax.rem(d + j, nd), peer[k], z),
                    device_id_type=MESH,
                )
                peers += 1
        for r in range(1, nz):
            pl.semaphore_signal(
                barrier, inc=1, device_id=(d, e, lax.rem(z + r, nz)), device_id_type=MESH
            )
            peers += 1
        for c in loads[:4]:
            c.start()

        row = lax.broadcasted_iota(jnp.int32, (lanes, tokens), 0)
        group = row // CAP
        slot = row - group * CAP
        label = jnp.zeros((lanes, tokens), jnp.int32)
        for k in range(ne):
            label = jnp.where(group == k, peer[k], label)
        chosen = jnp.zeros((lanes, tokens), F32)
        scale = jnp.zeros((lanes, tokens), F32)
        settle(routes, ld_sem.at[0])
        settle(combine, ld_sem.at[1])
        for c in range(top):
            hit = routes[c : c + 1, :] == label
            chosen = chosen + jnp.where(hit, 1.0, 0.0)
            scale = scale + jnp.where(hit, combine[c : c + 1, :], 0.0)
        row_id = lax.broadcasted_iota(jnp.int32, (tokens, tokens), 0)
        col_id = lax.broadcasted_iota(jnp.int32, (tokens, tokens), 1)
        upper = jnp.where(row_id < col_id, 1.0, 0.0).astype(BF16)
        before = dot(chosen.astype(BF16), upper, 1, 0)
        keep = jnp.logical_and(chosen > 0.0, before == slot.astype(F32))
        pick_f = jnp.where(keep, 1.0, 0.0)
        pick = pick_f.astype(BF16)
        factor = jnp.sum(pick_f * scale, axis=1, keepdims=True)
        pick_ref[...] = pick

        for c in loads[4:]:
            c.start()
        settle(tok, ld_sem.at[2])

        def dispatch(k, j, c):
            lo, hi = sent[group_of[k]][c]
            span = pl.ds(lo, hi - lo)
            return pltpu.make_async_remote_copy(
                src_ref=send.at[k * nd + j - 1, :, span], dst_ref=recv.at[k, d, :, span],
                send_sem=d_send.at[0], recv_sem=d_recv.at[group_of[k], c],
                device_id=(lax.rem(d + j, nd), peer[k], z), device_id_type=MESH,
            )

        far = range(groups[last][0], ne)

        def send_rows(ks, js):
            for k in ks:
                for c in range(len(sent[group_of[k]])):
                    for j in js:
                        if j or k:
                            dispatch(k, j, c).start()

        for j in range(nd - 1, -1, -1):
            dj = lax.rem(d + j, nd)
            span = pl.ds(pl.multiple_of(dj * half, 128), half)
            in_pick = dot(pick, tok[0, :, span], 1, 0)
            gr_pick = dot(pick, tok[1, :, span], 1, 0) * factor
            for k in range(ne):
                at = k * CAP
                tile = jnp.concatenate(
                    [in_pick[at : at + CAP], gr_pick[at : at + CAP]], axis=0
                ).astype(BF16)
                if j == 0 and k == 0:
                    recv[0, d] = tile
                else:
                    send[k * nd + j - 1] = tile
            if j == nd - 1:
                pl.semaphore_wait(barrier, peers)
            send_rows(range(far[0]), [j])
        settle(dw, ld_sem.at[3])
        dw_t[...] = dw[...].T
        settle(w2, ld_sem.at[4])

        def take(v, which):
            n = v.shape[0] // (2 * CAP)
            return v.reshape(n, 2, CAP, hidden)[:, which].reshape(n * CAP, hidden)

        def exchange(g, j):
            lo, hi = (k * nd * CAP for k in groups[g])
            span = pl.ds(lo, hi - lo)
            return pltpu.make_async_remote_copy(
                src_ref=psend.at[:, span], dst_ref=precv.at[j - 1, :, span],
                send_sem=p_send.at[0], recv_sem=p_recv.at[g],
                device_id=(lax.rem(d + j, nd), e, z), device_id_type=MESH,
            )

        def project(g):
            k0, k1 = groups[g]
            rows = (k1 - k0) * nd * 2 * CAP
            sums = [jnp.zeros((rows, hidden), F32)] * 3
            for c, (lo, hi) in enumerate(sent[g]):
                span = pl.ds(lo, hi - lo)
                if g:
                    settle(recv.at[pl.ds(k0, k1 - k0), :, :, span], d_recv.at[g, c])
                else:
                    for j in range(1, nd):
                        settle(recv.at[0, lax.rem(d + j, nd), :, span], d_recv.at[0, c])
                x = recv[k0:k1, :, :, lo:hi].reshape(rows, hi - lo)
                for i, w in enumerate((w2.at[0], w2.at[1], dw_t)):
                    sums[i] = sums[i] + dot(x, w[lo:hi, :], 1, 0)
            sums = [take(v, i // 2) for i, v in enumerate(sums)]
            lo, hi = k0 * nd * CAP, k1 * nd * CAP
            for i, v in enumerate(sums):
                psend[i, lo:hi] = v.astype(BF16)
            for j in range(1, nd):
                exchange(g, j).start()
            return sums

        def term_copy(k, s, c):
            lo, hi = back[group_of[k]][c]
            span = pl.ds(lo, hi - lo)
            return pltpu.make_async_remote_copy(
                src_ref=rowg.at[k, s, :, span], dst_ref=terms.at[z, k, :, span],
                send_sem=r_send.at[nd if k else s], recv_sem=r_recv.at[group_of[k], c],
                device_id=(s, peer[k], nd * s + d), device_id_type=MESH,
            )

        def own_copy(s, c):
            lo, hi = back[0][c]
            span = pl.ds(lo, hi - lo)
            return pltpu.make_async_copy(
                rowg.at[0, s, :, span], terms.at[z, 0, :, span], r_recv.at[0, c]
            )

        def is_own(s):
            return jnp.logical_and(d == s, z == nd * s + d)

        def finish(g, sums):
            k0, k1 = groups[g]
            lo, hi = k0 * nd * CAP, k1 * nd * CAP
            gate, up, dhid = sums
            settle(precv.at[:, :, pl.ds(lo, hi - lo)], p_recv.at[g])
            for j in range(1, nd):
                gate = gate + precv[j - 1, 0, lo:hi].astype(F32)
                up = up + precv[j - 1, 1, lo:hi].astype(F32)
                dhid = dhid + precv[j - 1, 2, lo:hi].astype(F32)
            sigma = jax.nn.sigmoid(gate)
            silu = gate * sigma
            act = silu * up
            d_up = dhid * silu
            d_gate = dhid * up * sigma * (1.0 + gate * (1.0 - sigma))
            both = jnp.concatenate([d_gate.astype(BF16), d_up.astype(BF16)], axis=1)
            for c, (at, to) in enumerate(back[g]):
                grad = dot(both, back_t[:, at:to], 1, 0)
                grad = grad.reshape(k1 - k0, nd, CAP, to - at).astype(BF16)
                for k in range(k0, k1):
                    for s in range(nd):
                        rowg[k, s, :, at:to] = grad[k - k0, s]
                        if k:
                            term_copy(k, s, c).start()
                            continue

                        @pl.when(is_own(s))
                        def _():
                            own_copy(s, c).start()

                        @pl.when(jnp.logical_not(is_own(s)))
                        def _():
                            term_copy(0, s, c).start()
            for i, v in enumerate((d_gate, d_up, act)):
                v = v.reshape((k1 - k0) * nd, CAP, hidden)
                zero = jnp.zeros_like(v)
                pair = [zero, v] if i == 2 else [v, zero]
                pads[i, k0 * nd : k1 * nd] = jnp.concatenate(pair, axis=1).astype(BF16)

        def gather(g, r, c):
            k0, k1 = groups[g]
            lo, hi = back[g][c]
            ref = agbuf.at[part, pl.ds(k0, k1 - k0), :, pl.ds(lo, hi - lo)]
            return pltpu.make_async_remote_copy(
                src_ref=ref, dst_ref=ref,
                send_sem=a_send.at[0], recv_sem=a_recv.at[0],
                device_id=(d, e, lax.rem(z + r, nz)), device_id_type=MESH,
            )

        def reduce(g):
            k0, k1 = groups[g]

            @pl.when(reducer)
            def _():
                for c, (lo, hi) in enumerate(back[g]):
                    settle(terms.at[:, pl.ds(k0, k1 - k0), :, pl.ds(lo, hi - lo)], r_recv.at[g, c])
                    total = terms[0, k0:k1, :, lo:hi].astype(F32)
                    for q in range(1, nz):
                        total = total + terms[q, k0:k1, :, lo:hi].astype(F32)
                    agbuf[part, k0:k1, :, lo:hi] = total.astype(BF16)
                    for r in range(1, nz):
                        gather(g, r, c).start()

        every = ne * nd * 2 * CAP

        def weight_grad(i):
            x = recv[...].reshape(every, half)
            v = pads[i].reshape(every, hidden)
            if i == 2:
                gd_ref[0] = (dot(v, x, 0, 0) * 0.25).astype(BF16)
            else:
                (gg_ref, gu_ref)[i][0] = (dot(x, v, 0, 0) * 0.25).astype(BF16)

        for g in range(len(groups)):
            if g == last:
                for h in range(last - 1):
                    reduce(h)
            sums = project(g)
            if g == 0:
                back_t[:hidden] = w2[0].T
                back_t[hidden:] = w2[1].T
                send_rows(far, range(nd - 1, -1, -1))
            finish(g, sums)
        for i in range(3):
            weight_grad(i)
        settle(send, d_send.at[0])
        settle(precv, p_send.at[0])
        settle(rowg.at[pl.ds(1, ne - 1)], r_send.at[nd])
        for s in range(nd):
            @pl.when(jnp.logical_not(is_own(s)))
            def _():
                settle(rowg.at[0, s], r_send.at[s])

        for h in range(max(last - 1, 0), last + 1):
            reduce(h)

        @pl.when(jnp.logical_not(reducer))
        def _():
            settle(agbuf, a_recv.at[0])

        @pl.when(reducer)
        def _():
            settle(agbuf.at[pl.ds(0, nd - 1)], a_recv.at[0])
            settle(terms.at[pl.ds(0, nz - 1)], a_send.at[0])

    return kernel


def make_store(nd, lanes, half):
    parts = [(h, lo, hi) for h in range(nd) for lo, hi in cuts(half, STORE_PARTS // nd)]

    def kernel(agbuf, pick_ref, gg, gu, gd, out, gg_out, gu_out, gd_out, out_v, sem, out_sem):
        copies = [
            pltpu.make_async_copy(src, dst, sem.at[i])
            for i, (src, dst) in enumerate(((gg, gg_out), (gu, gu_out), (gd, gd_out)))
        ]
        for c in copies:
            c.start()
        pick = pick_ref[...]
        for i, (h, lo, hi) in enumerate(parts):
            got = agbuf[h, :, :, lo:hi].astype(F32).reshape(lanes, hi - lo).astype(BF16)
            span = pl.ds(h * half + lo, hi - lo)
            out_v[:, span] = dot(pick, got, 0, 0).astype(BF16)
            c = pltpu.make_async_copy(out_v.at[:, span], out.at[:, span], out_sem.at[i])
            c.start()
            copies.append(c)
        for c in copies:
            c.wait()

    return kernel, len(parts)


def body(grad_out, layer_in, routes, combine, gate_weight, up_weight, down_weight):
    nd = lax.axis_size("dp")
    ne = lax.axis_size("expert")
    nz = lax.axis_size("tensor")
    tokens, width = grad_out.shape
    top = routes.shape[1]
    half, hidden = gate_weight.shape[1:]
    lanes = ne * CAP
    groups = len(group_ranges(ne))
    kernel = make_kernel(nd, ne, nz, tokens, width, half, hidden, top)
    hbm = pl.BlockSpec(memory_space=pltpu.HBM)
    vmem = pl.BlockSpec(memory_space=pltpu.VMEM)
    dma = pltpu.SemaphoreType.DMA
    held = 2 * (nd * lanes * half + lanes * tokens + 3 * half * hidden)
    room = VMEM - held
    arrays = pl.pallas_call(
        kernel,
        out_shape=(
            pltpu.VMEM((nd, ne, CAP, half), BF16),
            pltpu.VMEM((lanes, tokens), BF16),
            pltpu.VMEM(gate_weight.shape, BF16),
            pltpu.VMEM(up_weight.shape, BF16),
            pltpu.VMEM(down_weight.shape, BF16),
        ),
        in_specs=[hbm] * 7,
        out_specs=(vmem,) * 5,
        scratch_shapes=[
            pltpu.VMEM((2, tokens, width), BF16),
            pltpu.VMEM((top, tokens), jnp.int32),
            pltpu.VMEM((top, tokens), F32),
            pltpu.VMEM((2, half, hidden), BF16),
            pltpu.VMEM((hidden, half), BF16),
            pltpu.VMEM((half, hidden), BF16),
            pltpu.VMEM((2 * hidden, half), BF16),
            pltpu.VMEM((ne * nd - 1, 2 * CAP, half), BF16),
            pltpu.VMEM((ne, nd, 2 * CAP, half), BF16),
            pltpu.VMEM((3, ne * nd * CAP, hidden), BF16),
            pltpu.VMEM((nd - 1, 3, ne * nd * CAP, hidden), BF16),
            pltpu.VMEM((ne, nd, CAP, half), BF16),
            pltpu.VMEM((nz, ne, CAP, half), BF16),
            pltpu.VMEM((3, ne * nd, 2 * CAP, hidden), BF16),
            dma((5,)),
            dma((1,)),
            dma((groups, FAR_PARTS)),
            dma((1,)),
            dma((groups,)),
            dma((nd + 1,)),
            dma((groups, max(BACK_PARTS))),
            dma((1,)),
            dma((1,)),
        ],
        compiler_params=pltpu.CompilerParams(
            collective_id=0, has_side_effects=True, vmem_limit_bytes=room
        ),
    )(grad_out, layer_in, routes.T, combine.T, gate_weight, up_weight, down_weight)
    store, parts = make_store(nd, lanes, half)
    return tuple(pl.pallas_call(
        store,
        out_shape=tuple(
            jax.ShapeDtypeStruct(v.shape, BF16)
            for v in (grad_out, gate_weight, up_weight, down_weight)
        ),
        in_specs=[vmem] * 5,
        out_specs=(hbm,) * 4,
        scratch_shapes=[pltpu.VMEM((tokens, width), BF16), dma((3,)), dma((parts,))],
        compiler_params=pltpu.CompilerParams(vmem_limit_bytes=16 * 2**20),
    )(*[pltpu.with_memory_space_constraint(a, pltpu.VMEM) for a in arrays]))


def solution(mesh):
    return jax.shard_map(
        body,
        mesh=mesh,
        in_specs=(
            P(("dp", "expert"), None),
            P(("dp", "expert"), None),
            P(("dp", "expert"), None),
            P(("dp", "expert"), None),
            P("expert", "dp", "tensor"),
            P("expert", "dp", "tensor"),
            P("expert", "tensor", "dp"),
        ),
        out_specs=(
            P(("dp", "expert"), None),
            P("expert", "dp", "tensor"),
            P("expert", "dp", "tensor"),
            P("expert", "tensor", "dp"),
        ),
        check_vma=False,
    )
```

```python
import jax
import jax.numpy as jnp
from jax import lax
from jax.experimental import pallas as pl
from jax.experimental.pallas import tpu as pltpu
from jax.sharding import PartitionSpec as P

CAP = 8
BACK_PARTS = (1, 2, 2)
FAR_PARTS = 2
STORE_PARTS = 4
VMEM = 67043328
MESH = pl.DeviceIdType.MESH
F32 = jnp.float32
BF16 = jnp.bfloat16


def dot(a, b, ca, cb):
    return lax.dot_general(a, b, (((ca,), (cb,)), ((), ())), preferred_element_type=F32)


def cuts(extent, parts):
    tiles = extent // 128
    edges = [128 * ((tiles * c + parts - 1) // parts) for c in range(parts + 1)]
    return list(zip(edges[:-1], edges[1:]))


def partner(e, k, ne):
    out, bit = 0, 1
    while bit < ne:
        own = lax.rem(lax.div(e, bit), 2)
        out = out + bit * ((1 - own) if k & bit else own)
        bit *= 2
    return out


def group_ranges(ne):
    edges = sorted({0, 1, 3 * ne // 4, ne})
    return list(zip(edges[:-1], edges[1:]))


def make_kernel(nd, ne, nz, tokens, width, half, hidden, top):
    lanes = ne * CAP
    groups = group_ranges(ne)
    last = len(groups) - 1
    group_of = [g for g, (k0, k1) in enumerate(groups) for _ in range(k0, k1)]
    back = [cuts(half, BACK_PARTS[min(g, 2)]) for g in range(len(groups))]
    sent = [cuts(half, FAR_PARTS if g == last else 1) for g in range(len(groups))]

    def kernel(
        go_hbm, li_hbm, routes_hbm, combine_hbm, gw_hbm, uw_hbm, dw_hbm,
        agbuf, pick_ref, gg_ref, gu_ref, gd_ref,
        tok, routes, combine, w2, dw, dw_t, back_t, send, recv, psend, precv, rowg, terms, pads,
        ld_sem, d_send, d_recv, p_send, p_recv, r_send, r_recv, a_send, a_recv,
    ):
        d = lax.axis_index("dp")
        e = lax.axis_index("expert")
        z = lax.axis_index("tensor")
        peer = [partner(e, k, ne) for k in range(ne)]
        part = z - (nd * d)
        reducer = jnp.logical_and(part >= 0, part < nd)

        loads = [
            pltpu.make_async_copy(routes_hbm, routes, ld_sem.at[0]),
            pltpu.make_async_copy(combine_hbm, combine, ld_sem.at[1]),
            pltpu.make_async_copy(li_hbm, tok.at[0], ld_sem.at[2]),
            pltpu.make_async_copy(go_hbm, tok.at[1], ld_sem.at[2]),
            pltpu.make_async_copy(dw_hbm.at[0], dw, ld_sem.at[3]),
            pltpu.make_async_copy(gw_hbm.at[0], w2.at[0], ld_sem.at[4]),
            pltpu.make_async_copy(uw_hbm.at[0], w2.at[1], ld_sem.at[4]),
        ]

        def settle(ref, sem):
            pltpu.make_async_copy(ref, ref, sem).wait()

        barrier = pltpu.get_barrier_semaphore()
        peers = 0
        for k in range(ne - 1, -1, -1):
            for j in range(nd):
                if j == 0 and k == 0:
                    continue
                pl.semaphore_signal(
                    barrier, inc=1, device_id=(lax.rem(d + j, nd), peer[k], z),
                    device_id_type=MESH,
                )
                peers += 1
        for r in range(1, nz):
            pl.semaphore_signal(
                barrier, inc=1, device_id=(d, e, lax.rem(z + r, nz)), device_id_type=MESH
            )
            peers += 1
        for c in loads:
            c.start()

        row = lax.broadcasted_iota(jnp.int32, (lanes, tokens), 0)
        group = row // CAP
        slot = row - group * CAP
        label = jnp.zeros((lanes, tokens), jnp.int32)
        for k in range(ne):
            label = jnp.where(group == k, peer[k], label)
        chosen = jnp.zeros((lanes, tokens), F32)
        scale = jnp.zeros((lanes, tokens), F32)
        settle(routes, ld_sem.at[0])
        settle(combine, ld_sem.at[1])
        for c in range(top):
            hit = routes[c : c + 1, :] == label
            chosen = chosen + jnp.where(hit, 1.0, 0.0)
            scale = scale + jnp.where(hit, combine[c : c + 1, :], 0.0)
        row_id = lax.broadcasted_iota(jnp.int32, (tokens, tokens), 0)
        col_id = lax.broadcasted_iota(jnp.int32, (tokens, tokens), 1)
        upper = jnp.where(row_id < col_id, 1.0, 0.0).astype(BF16)
        before = dot(chosen.astype(BF16), upper, 1, 0)
        keep = jnp.logical_and(chosen > 0.0, before == slot.astype(F32))
        pick_f = jnp.where(keep, 1.0, 0.0)
        pick = pick_f.astype(BF16)
        factor = jnp.sum(pick_f * scale, axis=1, keepdims=True)
        pick_ref[...] = pick

        settle(tok, ld_sem.at[2])

        def dispatch(k, j, c):
            lo, hi = sent[group_of[k]][c]
            span = pl.ds(lo, hi - lo)
            return pltpu.make_async_remote_copy(
                src_ref=send.at[k * nd + j - 1, :, span], dst_ref=recv.at[k, d, :, span],
                send_sem=d_send.at[0], recv_sem=d_recv.at[group_of[k], c],
                device_id=(lax.rem(d + j, nd), peer[k], z), device_id_type=MESH,
            )

        for j in range(nd - 1, -1, -1):
            dj = lax.rem(d + j, nd)
            span = pl.ds(pl.multiple_of(dj * half, 128), half)
            in_pick = dot(pick, tok[0, :, span], 1, 0)
            gr_pick = dot(pick, tok[1, :, span], 1, 0) * factor
            for k in range(ne):
                at = k * CAP
                tile = jnp.concatenate(
                    [in_pick[at : at + CAP], gr_pick[at : at + CAP]], axis=0
                ).astype(BF16)
                if j == 0 and k == 0:
                    recv[0, d] = tile
                else:
                    send[k * nd + j - 1] = tile
        pl.semaphore_wait(barrier, peers)
        def send_rows(ks):
            for k in ks:
                for c in range(len(sent[group_of[k]])):
                    for j in range(nd - 1, -1, -1):
                        if j or k:
                            dispatch(k, j, c).start()

        far = range(groups[last][0], ne)
        send_rows(range(far[0]))
        settle(dw, ld_sem.at[3])
        dw_t[...] = dw[...].T
        settle(w2, ld_sem.at[4])

        def take(v, which):
            n = v.shape[0] // (2 * CAP)
            return v.reshape(n, 2, CAP, hidden)[:, which].reshape(n * CAP, hidden)

        def exchange(g, j):
            lo, hi = (k * nd * CAP for k in groups[g])
            span = pl.ds(lo, hi - lo)
            return pltpu.make_async_remote_copy(
                src_ref=psend.at[:, span], dst_ref=precv.at[j - 1, :, span],
                send_sem=p_send.at[0], recv_sem=p_recv.at[g],
                device_id=(lax.rem(d + j, nd), e, z), device_id_type=MESH,
            )

        def project(g):
            k0, k1 = groups[g]
            rows = (k1 - k0) * nd * 2 * CAP
            sums = [jnp.zeros((rows, hidden), F32)] * 3
            for c, (lo, hi) in enumerate(sent[g]):
                span = pl.ds(lo, hi - lo)
                if g:
                    settle(recv.at[pl.ds(k0, k1 - k0), :, :, span], d_recv.at[g, c])
                else:
                    for j in range(1, nd):
                        settle(recv.at[0, lax.rem(d + j, nd), :, span], d_recv.at[0, c])
                x = recv[k0:k1, :, :, lo:hi].reshape(rows, hi - lo)
                for i, w in enumerate((w2.at[0], w2.at[1], dw_t)):
                    sums[i] = sums[i] + dot(x, w[lo:hi, :], 1, 0)
            sums = [take(v, i // 2) for i, v in enumerate(sums)]
            lo, hi = k0 * nd * CAP, k1 * nd * CAP
            for i, v in enumerate(sums):
                psend[i, lo:hi] = v.astype(BF16)
            for j in range(1, nd):
                exchange(g, j).start()
            return sums

        def term_copy(k, s, c):
            lo, hi = back[group_of[k]][c]
            span = pl.ds(lo, hi - lo)
            return pltpu.make_async_remote_copy(
                src_ref=rowg.at[k, s, :, span], dst_ref=terms.at[z, k, :, span],
                send_sem=r_send.at[nd if k else s], recv_sem=r_recv.at[group_of[k], c],
                device_id=(s, peer[k], nd * s + d), device_id_type=MESH,
            )

        def own_copy(s, c):
            lo, hi = back[0][c]
            span = pl.ds(lo, hi - lo)
            return pltpu.make_async_copy(
                rowg.at[0, s, :, span], terms.at[z, 0, :, span], r_recv.at[0, c]
            )

        def is_own(s):
            return jnp.logical_and(d == s, z == nd * s + d)

        def finish(g, sums):
            k0, k1 = groups[g]
            lo, hi = k0 * nd * CAP, k1 * nd * CAP
            gate, up, dhid = sums
            settle(precv.at[:, :, pl.ds(lo, hi - lo)], p_recv.at[g])
            for j in range(1, nd):
                gate = gate + precv[j - 1, 0, lo:hi].astype(F32)
                up = up + precv[j - 1, 1, lo:hi].astype(F32)
                dhid = dhid + precv[j - 1, 2, lo:hi].astype(F32)
            sigma = jax.nn.sigmoid(gate)
            silu = gate * sigma
            act = silu * up
            d_up = dhid * silu
            d_gate = dhid * up * sigma * (1.0 + gate * (1.0 - sigma))
            both = jnp.concatenate([d_gate.astype(BF16), d_up.astype(BF16)], axis=1)
            for c, (at, to) in enumerate(back[g]):
                grad = dot(both, back_t[:, at:to], 1, 0)
                grad = grad.reshape(k1 - k0, nd, CAP, to - at).astype(BF16)
                for k in range(k0, k1):
                    for s in range(nd):
                        rowg[k, s, :, at:to] = grad[k - k0, s]
                        if k:
                            term_copy(k, s, c).start()
                            continue

                        @pl.when(is_own(s))
                        def _():
                            own_copy(s, c).start()

                        @pl.when(jnp.logical_not(is_own(s)))
                        def _():
                            term_copy(0, s, c).start()
            for i, v in enumerate((d_gate, d_up, act)):
                v = v.reshape((k1 - k0) * nd, CAP, hidden)
                zero = jnp.zeros_like(v)
                pair = [zero, v] if i == 2 else [v, zero]
                pads[i, k0 * nd : k1 * nd] = jnp.concatenate(pair, axis=1).astype(BF16)

        def gather(g, r, c):
            k0, k1 = groups[g]
            lo, hi = back[g][c]
            ref = agbuf.at[part, pl.ds(k0, k1 - k0), :, pl.ds(lo, hi - lo)]
            return pltpu.make_async_remote_copy(
                src_ref=ref, dst_ref=ref,
                send_sem=a_send.at[0], recv_sem=a_recv.at[0],
                device_id=(d, e, lax.rem(z + r, nz)), device_id_type=MESH,
            )

        def reduce(g):
            k0, k1 = groups[g]

            @pl.when(reducer)
            def _():
                for c, (lo, hi) in enumerate(back[g]):
                    settle(terms.at[:, pl.ds(k0, k1 - k0), :, pl.ds(lo, hi - lo)], r_recv.at[g, c])
                    total = terms[0, k0:k1, :, lo:hi].astype(F32)
                    for q in range(1, nz):
                        total = total + terms[q, k0:k1, :, lo:hi].astype(F32)
                    agbuf[part, k0:k1, :, lo:hi] = total.astype(BF16)
                    for r in range(1, nz):
                        gather(g, r, c).start()

        every = ne * nd * 2 * CAP

        def weight_grad(i):
            x = recv[...].reshape(every, half)
            v = pads[i].reshape(every, hidden)
            if i == 2:
                gd_ref[0] = (dot(v, x, 0, 0) * 0.25).astype(BF16)
            else:
                (gg_ref, gu_ref)[i][0] = (dot(x, v, 0, 0) * 0.25).astype(BF16)

        for g in range(len(groups)):
            if g == last:
                for h in range(last - 1):
                    reduce(h)
            sums = project(g)
            if g == 0:
                back_t[:hidden] = w2[0].T
                back_t[hidden:] = w2[1].T
                send_rows(far)
            finish(g, sums)
        for i in range(3):
            weight_grad(i)
        settle(send, d_send.at[0])
        settle(precv, p_send.at[0])
        settle(rowg.at[pl.ds(1, ne - 1)], r_send.at[nd])
        for s in range(nd):
            @pl.when(jnp.logical_not(is_own(s)))
            def _():
                settle(rowg.at[0, s], r_send.at[s])

        for h in range(max(last - 1, 0), last + 1):
            reduce(h)

        @pl.when(jnp.logical_not(reducer))
        def _():
            settle(agbuf, a_recv.at[0])

        @pl.when(reducer)
        def _():
            settle(agbuf.at[pl.ds(0, nd - 1)], a_recv.at[0])
            settle(terms.at[pl.ds(0, nz - 1)], a_send.at[0])

    return kernel


def make_store(nd, lanes, half):
    parts = [(h, lo, hi) for h in range(nd) for lo, hi in cuts(half, STORE_PARTS // nd)]

    def kernel(agbuf, pick_ref, gg, gu, gd, out, gg_out, gu_out, gd_out, out_v, sem, out_sem):
        copies = [
            pltpu.make_async_copy(src, dst, sem.at[i])
            for i, (src, dst) in enumerate(((gg, gg_out), (gu, gu_out), (gd, gd_out)))
        ]
        for i, c in enumerate(copies):
            c.start(priority=i % 2)
        pick = pick_ref[...]
        for i, (h, lo, hi) in enumerate(parts):
            got = agbuf[h, :, :, lo:hi].astype(F32).reshape(lanes, hi - lo).astype(BF16)
            span = pl.ds(h * half + lo, hi - lo)
            out_v[:, span] = dot(pick, got, 0, 0).astype(BF16)
            c = pltpu.make_async_copy(out_v.at[:, span], out.at[:, span], out_sem.at[i])
            c.start(priority=1)
            copies.append(c)
        for c in copies:
            c.wait()

    return kernel, len(parts)


def body(grad_out, layer_in, routes, combine, gate_weight, up_weight, down_weight):
    nd = lax.axis_size("dp")
    ne = lax.axis_size("expert")
    nz = lax.axis_size("tensor")
    tokens, width = grad_out.shape
    top = routes.shape[1]
    half, hidden = gate_weight.shape[1:]
    lanes = ne * CAP
    groups = len(group_ranges(ne))
    kernel = make_kernel(nd, ne, nz, tokens, width, half, hidden, top)
    hbm = pl.BlockSpec(memory_space=pltpu.HBM)
    vmem = pl.BlockSpec(memory_space=pltpu.VMEM)
    dma = pltpu.SemaphoreType.DMA
    held = 2 * (nd * lanes * half + lanes * tokens + 3 * half * hidden)
    room = VMEM - held
    arrays = pl.pallas_call(
        kernel,
        out_shape=(
            pltpu.VMEM((nd, ne, CAP, half), BF16),
            pltpu.VMEM((lanes, tokens), BF16),
            pltpu.VMEM(gate_weight.shape, BF16),
            pltpu.VMEM(up_weight.shape, BF16),
            pltpu.VMEM(down_weight.shape, BF16),
        ),
        in_specs=[hbm] * 7,
        out_specs=(vmem,) * 5,
        scratch_shapes=[
            pltpu.VMEM((2, tokens, width), BF16),
            pltpu.VMEM((top, tokens), jnp.int32),
            pltpu.VMEM((top, tokens), F32),
            pltpu.VMEM((2, half, hidden), BF16),
            pltpu.VMEM((hidden, half), BF16),
            pltpu.VMEM((half, hidden), BF16),
            pltpu.VMEM((2 * hidden, half), BF16),
            pltpu.VMEM((ne * nd - 1, 2 * CAP, half), BF16),
            pltpu.VMEM((ne, nd, 2 * CAP, half), BF16),
            pltpu.VMEM((3, ne * nd * CAP, hidden), BF16),
            pltpu.VMEM((nd - 1, 3, ne * nd * CAP, hidden), BF16),
            pltpu.VMEM((ne, nd, CAP, half), BF16),
            pltpu.VMEM((nz, ne, CAP, half), BF16),
            pltpu.VMEM((3, ne * nd, 2 * CAP, hidden), BF16),
            dma((5,)),
            dma((1,)),
            dma((groups, FAR_PARTS)),
            dma((1,)),
            dma((groups,)),
            dma((nd + 1,)),
            dma((groups, max(BACK_PARTS))),
            dma((1,)),
            dma((1,)),
        ],
        compiler_params=pltpu.CompilerParams(
            collective_id=0, has_side_effects=True, vmem_limit_bytes=room
        ),
    )(grad_out, layer_in, routes.T, combine.T, gate_weight, up_weight, down_weight)
    store, parts = make_store(nd, lanes, half)
    return tuple(pl.pallas_call(
        store,
        out_shape=tuple(
            jax.ShapeDtypeStruct(v.shape, BF16)
            for v in (grad_out, gate_weight, up_weight, down_weight)
        ),
        in_specs=[vmem] * 5,
        out_specs=(hbm,) * 4,
        scratch_shapes=[pltpu.VMEM((tokens, width), BF16), dma((3,)), dma((parts,))],
        compiler_params=pltpu.CompilerParams(vmem_limit_bytes=16 * 2**20),
    )(*[pltpu.with_memory_space_constraint(a, pltpu.VMEM) for a in arrays]))


def solution(mesh):
    return jax.shard_map(
        body,
        mesh=mesh,
        in_specs=(
            P(("dp", "expert"), None),
            P(("dp", "expert"), None),
            P(("dp", "expert"), None),
            P(("dp", "expert"), None),
            P("expert", "dp", "tensor"),
            P("expert", "dp", "tensor"),
            P("expert", "tensor", "dp"),
        ),
        out_specs=(
            P(("dp", "expert"), None),
            P("expert", "dp", "tensor"),
            P("expert", "dp", "tensor"),
            P("expert", "tensor", "dp"),
        ),
        check_vma=False,
    )
```
